32 devices in a mesh: dp: 8 (over z, x), tensor: 4 (over y, core).
Axes of the slice: x: 2, y: 2, z: 4, core: 2. Of those that a mesh axis runs over, the one named last changes fastest.
Arguments:
- tokens: bfloat16 [3072, 768], P('dp'), may hold values from -6 to 6
- segment_ids: int32 [3072], P('dp'), may hold values from -1 to 7, as said below
- cotangent: bfloat16 [3072, 768], P('dp'), may hold values from -6 to 6
- attn_input: bfloat16 [3, 768, 768], P(None, None, 'tensor'), may hold values from -3 to 3, as said below
- query_bias: float32 [768], P('tensor'), may hold values from -3 to 3
- value_bias: float32 [768], P('tensor'), may hold values from -3 to 3
- attn_output: bfloat16 [768, 768], P('tensor'), may hold values from -2 to 2
- output_bias: float32 [768], replicated, may hold values from -2 to 2
- gain_first: float32 [768], replicated, may hold values from 0.25 to 1.75
- shift_first: float32 [768], replicated, may hold values from -2 to 2
- hidden_weight: bfloat16 [768, 3072], P(None, 'tensor'), may hold values from -0.21875 to 0.21875
- hidden_bias: float32 [3072], P('tensor'), may hold values from -3 to 3
- down_weight: bfloat16 [3072, 768], P('tensor'), may hold values from -0.109375 to 0.109375
- down_bias: float32 [768], replicated, may hold values from -2 to 2
- gain_second: float32 [768], replicated, may hold values from 0.25 to 1.75
- shift_second: float32 [768], replicated, may hold values from -2 to 2
Outputs:
- block_out: bfloat16 [3072, 768], P('dp')
- input_grad: bfloat16 [3072, 768], P('dp')
- grad_attn_input: float32 [3, 768, 768], P(None, None, 'tensor')
- grad_query_bias: float32 [768], P('tensor')
- grad_value_bias: float32 [768], P('tensor')
- grad_attn_output: float32 [768, 768], P('tensor')
- grad_output_bias: float32 [768], replicated
- grad_gain_first: float32 [768], replicated
- grad_shift_first: float32 [768], replicated
- grad_hidden_weight: float32 [768, 3072], P(None, 'tensor')
- grad_hidden_bias: float32 [3072], P('tensor')
- grad_down_weight: float32 [3072, 768], P('tensor')
- grad_down_bias: float32 [768], replicated
- grad_gain_second: float32 [768], replicated
- grad_shift_second: float32 [768], replicated
The draws below stay inside these ranges and needn't reach their ends.
Inputs may be any that keep to these rules, and one draw needn't show every extreme that they name: `segment_ids`: block g of 384 slots (the slots of one index of dp) begins with one sequence of id g, of 192 to 384 tokens; its remaining slots are padding with id -1. In every draw some block holds a sequence of 384 tokens. `attn_input`: entries of order D ** -0.5.
All inputs are finite; a program needn't handle non-finite values.
Results may differ from the reference program's by a relative error of at most 0.011.
Values sent between devices are 32-bit elements; how exact they have to be, the bound alone decides.
A program may use at most 128 MiB of HBM per device.

```python
import jax
import jax.numpy as jnp
from jax import lax

D = 768
HEADS = 12
HD = 64
FF = 3072
CAP = 384
MINSEQ = 192
TOKENS = 3072


def draw_segment_ids(key, part):
    groups = TOKENS // CAP
    key_length, key_forced = jax.random.split(jax.random.fold_in(key, 7), 2)
    lengths = jax.random.randint(key_length, (groups,), MINSEQ, CAP + 1)
    forced = jax.random.randint(key_forced, (), 0, groups)
    block_index = jnp.arange(groups)
    lengths = jnp.where(block_index == forced, CAP, lengths)
    position = jnp.arange(CAP)
    inside = position[None, :] < lengths[:, None]
    segment_table = jnp.where(inside, jnp.arange(groups, dtype=jnp.int32)[:, None], -1)
    return segment_table.reshape(TOKENS).astype(jnp.int32)


def draw_attn_input(key, part):
    base_key = jax.random.fold_in(jax.random.fold_in(key, 11), 0)
    base = jnp.clip(jax.random.normal(base_key, (3, D, D), jnp.float32), -4.0, 4.0) * D ** (-0.5)
    return base.astype(jnp.bfloat16)


def levels(stream_key, extent, shards, least, top_value):
    def one(axis_at, parts):
        steps = jax.random.uniform(jax.random.fold_in(jax.random.fold_in(stream_key, 6), axis_at), (parts,), jnp.float32, least / len(shards), top_value / len(shards))
        return jnp.repeat(jnp.exp(steps), extent[axis_at] // parts).reshape((-1,) + (1,) * (len(extent) - axis_at - 1))

    gain = one(*shards[0])
    for cut in shards[1:]:
        gain = gain * one(*cut)
    return gain


def bell_draw(stream_key, shape, scale, reach, cuts=(), kind=jnp.bfloat16):
    result = jax.random.normal(stream_key, shape, jnp.float32) * scale
    if len(cuts) > 0:
        result = levels(stream_key, shape, cuts, -0.22, 0.18) * result
    return jnp.clip(result, min=-reach, max=reach).astype(kind)


def setup_inputs(seed: int = 0) -> dict:
    splits = jax.random.split(jax.random.key(seed), 17)
    return {
        "tokens": bell_draw(splits[0], (TOKENS, D), 1.0, 6.0, ((0, 8),)),
        "segment_ids": draw_segment_ids(jax.random.fold_in(splits[16], 71), 0),
        "cotangent": bell_draw(splits[2], (TOKENS, D), 1.0, 6.0, ((0, 8),)),
        "attn_input": draw_attn_input(jax.random.fold_in(splits[16], 71), 0),
        "query_bias": bell_draw(splits[4], (D,), 0.5, 3.0, ((0, 4),), jnp.float32),
        "value_bias": bell_draw(splits[5], (D,), 0.5, 3.0, ((0, 4),), jnp.float32),
        "attn_output": bell_draw(splits[6], (D, D), (D * 4 // CAP) ** -0.5, 2.0, ((0, 4),)),
        "output_bias": bell_draw(splits[7], (D,), 0.3, 2.0, (), jnp.float32),
        "gain_first": jnp.clip(1.0 + 0.15 * jax.random.normal(splits[8], (D,), jnp.float32), 0.25, 1.75),
        "shift_first": bell_draw(splits[9], (D,), 0.3, 2.0, (), jnp.float32),
        "hidden_weight": bell_draw(splits[10], (D, FF), D ** -0.5, 0.21875, ((1, 4),)),
        "hidden_bias": bell_draw(splits[11], (FF,), 0.5, 3.0, ((0, 4),), jnp.float32),
        "down_weight": bell_draw(splits[12], (FF, D), FF ** -0.5, 0.109375, ((0, 4),)),
        "down_bias": bell_draw(splits[13], (D,), 0.3, 2.0, (), jnp.float32),
        "gain_second": jnp.clip(1.0 + 0.15 * jax.random.normal(splits[14], (D,), jnp.float32), 0.25, 1.75),
        "shift_second": bell_draw(splits[15], (D,), 0.3, 2.0, (), jnp.float32),
    }


EPSILON = 1e-05
TANH_SCALE = 0.7978845608028654
CUBIC = 0.044715

def norm_forward(values_in, norm_gain, norm_shift):
    row_mean = lax.optimization_barrier(jnp.mean(values_in, axis=-1, keepdims=True))
    centered = values_in - row_mean
    inverse = lax.rsqrt(lax.optimization_barrier(jnp.mean(centered * centered, axis=-1, keepdims=True)) + EPSILON)
    normed = centered * inverse
    return (normed, inverse, normed * norm_gain + norm_shift)

def norm_backward(grad_out, normed, inverse, norm_gain):
    scaled = grad_out * norm_gain
    return inverse * (scaled - lax.optimization_barrier(jnp.mean(scaled, axis=-1, keepdims=True)) - normed * lax.optimization_barrier(jnp.mean(scaled * normed, axis=-1, keepdims=True)))

def gelu_pair(pre_act):
    tangent = jnp.tanh(TANH_SCALE * (pre_act + CUBIC * pre_act * pre_act * pre_act))
    gelu_value = 0.5 * pre_act * (1.0 + tangent)
    gelu_slope = 0.5 * (1.0 + tangent) + 0.5 * pre_act * (1.0 - tangent * tangent) * TANH_SCALE * (1.0 + 3.0 * CUBIC * pre_act * pre_act)
    return (gelu_value, gelu_slope)

def allowed_mask(segments):
    position = jnp.arange(segments.shape[0])
    return (segments[:, None] == segments[None, :]) & (position[None, :] <= position[:, None])

def head_scores(queries, keys_bf, allowed):
    scaling = queries.shape[-1] ** (-0.5)
    scores = jnp.einsum('qhd,khd->hqk', queries.astype(jnp.float32), keys_bf.astype(jnp.float32)) * scaling
    return jnp.where(allowed[None], scores, -jnp.inf)

def attend(queries, keys_bf, values_bf, allowed):
    scores = head_scores(queries, keys_bf, allowed)
    top_score = lax.optimization_barrier(jnp.max(scores, axis=-1, keepdims=True))
    log_sum = top_score + jnp.log(lax.optimization_barrier(jnp.sum(jnp.exp(scores - top_score), axis=-1, keepdims=True)))
    probs = jnp.exp(scores - log_sum).astype(jnp.bfloat16)
    mixed = jnp.einsum('hqk,khd->qhd', probs.astype(jnp.float32), values_bf.astype(jnp.float32))
    return (mixed, log_sum)

def attend_back(queries, keys_bf, values_bf, allowed, log_sum, grad_mixed):
    probs_full = jnp.exp(head_scores(queries, keys_bf, allowed) - log_sum)
    probs_bf = probs_full.astype(jnp.bfloat16).astype(jnp.float32)
    grad_float = grad_mixed.astype(jnp.float32)
    grad_values = jnp.einsum('hqk,qhd->khd', probs_bf, grad_float)
    grad_probs = jnp.einsum('qhd,khd->hqk', grad_float, values_bf.astype(jnp.float32))
    scaling = queries.shape[-1] ** (-0.5)
    grad_scores = (probs_full * (grad_probs - lax.optimization_barrier(jnp.sum(probs_full * grad_probs, axis=-1, keepdims=True))) * scaling).astype(jnp.bfloat16).astype(jnp.float32)
    grad_queries = jnp.einsum('hqk,khd->qhd', grad_scores, keys_bf.astype(jnp.float32))
    grad_keys = jnp.einsum('hqk,qhd->khd', grad_scores, queries.astype(jnp.float32))
    return (grad_queries, grad_keys, grad_values)

def group_pass(token_block, segment_block, cot_raw, weights):
    attn_input, query_bias, value_bias, attn_output, output_bias, gain_first, shift_first, hidden_weight, hidden_bias, down_weight, down_bias, gain_second, shift_second = weights
    row_count = token_block.shape[0]
    valid = (segment_block >= 0)[:, None]
    cot_block = jnp.where(valid, cot_raw, jnp.zeros_like(cot_raw))
    allowed = allowed_mask(segment_block)
    resid_in = token_block.astype(jnp.float32)
    normed_one, inverse_one, pre_one = norm_forward(resid_in, gain_first, shift_first)
    hidden_one = pre_one.astype(jnp.bfloat16)
    queries = (jnp.dot(hidden_one, attn_input[0], preferred_element_type=jnp.float32) + query_bias).astype(jnp.bfloat16).reshape(row_count, HEADS, HD)
    keys_bf = jnp.dot(hidden_one, attn_input[1], preferred_element_type=jnp.float32).astype(jnp.bfloat16).reshape(row_count, HEADS, HD)
    values_bf = (jnp.dot(hidden_one, attn_input[2], preferred_element_type=jnp.float32) + value_bias).astype(jnp.bfloat16).reshape(row_count, HEADS, HD)
    mixed, log_sum = attend(queries, keys_bf, values_bf, allowed)
    attended = mixed.reshape(row_count, D).astype(jnp.bfloat16)
    middle = resid_in + jnp.dot(attended, attn_output, preferred_element_type=jnp.float32) + output_bias
    normed_two, inverse_two, pre_two = norm_forward(middle, gain_second, shift_second)
    hidden_two = pre_two.astype(jnp.bfloat16)
    pre_act = jnp.dot(hidden_two, hidden_weight, preferred_element_type=jnp.float32) + hidden_bias
    gelu_value, gelu_slope = gelu_pair(pre_act)
    activation = gelu_value.astype(jnp.bfloat16)
    out_full = middle + jnp.dot(activation, down_weight, preferred_element_type=jnp.float32) + down_bias
    out_block = jnp.where(valid, out_full, jnp.zeros_like(out_full)).astype(jnp.bfloat16)
    grad_top = cot_block.astype(jnp.float32)
    grad_down_bias = lax.optimization_barrier(jnp.sum(grad_top, axis=0))
    grad_down_weight = jnp.dot(activation.T, cot_block, preferred_element_type=jnp.float32)
    grad_pre = jnp.dot(cot_block, down_weight.T, preferred_element_type=jnp.float32) * gelu_slope
    grad_hidden_bias = lax.optimization_barrier(jnp.sum(grad_pre, axis=0))
    grad_pre_bf = grad_pre.astype(jnp.bfloat16)
    grad_hidden_weight = jnp.dot(hidden_two.T, grad_pre_bf, preferred_element_type=jnp.float32)
    grad_two = jnp.dot(grad_pre_bf, hidden_weight.T, preferred_element_type=jnp.float32)
    grad_gain_second = lax.optimization_barrier(jnp.sum(grad_two * normed_two, axis=0))
    grad_shift_second = lax.optimization_barrier(jnp.sum(grad_two, axis=0))
    grad_middle = grad_top + norm_backward(grad_two, normed_two, inverse_two, gain_second)
    grad_output_bias = lax.optimization_barrier(jnp.sum(grad_middle, axis=0))
    grad_middle_bf = grad_middle.astype(jnp.bfloat16)
    grad_attn_output = jnp.dot(attended.T, grad_middle_bf, preferred_element_type=jnp.float32)
    grad_attended = jnp.dot(grad_middle_bf, attn_output.T, preferred_element_type=jnp.float32).astype(jnp.bfloat16).reshape(row_count, HEADS, HD)
    grad_queries, grad_keys, grad_values = attend_back(queries, keys_bf, values_bf, allowed, log_sum, grad_attended)
    grad_queries = grad_queries.reshape(row_count, D)
    grad_keys = grad_keys.reshape(row_count, D)
    grad_values = grad_values.reshape(row_count, D)
    grad_query_bias = lax.optimization_barrier(jnp.sum(grad_queries, axis=0))
    grad_value_bias = lax.optimization_barrier(jnp.sum(grad_values, axis=0))
    query_bf = grad_queries.astype(jnp.bfloat16)
    key_grad_bf = grad_keys.astype(jnp.bfloat16)
    value_grad_bf = grad_values.astype(jnp.bfloat16)
    grad_attn_input = jnp.stack([jnp.dot(hidden_one.T, query_bf, preferred_element_type=jnp.float32), jnp.dot(hidden_one.T, key_grad_bf, preferred_element_type=jnp.float32), jnp.dot(hidden_one.T, value_grad_bf, preferred_element_type=jnp.float32)])
    grad_one = jnp.dot(query_bf, attn_input[0].T, preferred_element_type=jnp.float32) + jnp.dot(key_grad_bf, attn_input[1].T, preferred_element_type=jnp.float32) + jnp.dot(value_grad_bf, attn_input[2].T, preferred_element_type=jnp.float32)
    grad_gain_first = lax.optimization_barrier(jnp.sum(grad_one * normed_one, axis=0))
    grad_shift_first = lax.optimization_barrier(jnp.sum(grad_one, axis=0))
    grad_block = (grad_middle + norm_backward(grad_one, normed_one, inverse_one, gain_first)).astype(jnp.bfloat16)
    grads = (grad_attn_input, grad_query_bias, grad_value_bias, grad_attn_output, grad_output_bias, grad_gain_first, grad_shift_first, grad_hidden_weight, grad_hidden_bias, grad_down_weight, grad_down_bias, grad_gain_second, grad_shift_second)
    return (out_block, grad_block, grads)

def add_terms(left_term, right_term):
    return left_term + right_term

def reference(tokens, segment_ids, cotangent, attn_input, query_bias, value_bias, attn_output, output_bias, gain_first, shift_first, hidden_weight, hidden_bias, down_weight, down_bias, gain_second, shift_second):
    groups = TOKENS // CAP
    weights = (attn_input, query_bias, value_bias, attn_output, output_bias, gain_first, shift_first, hidden_weight, hidden_bias, down_weight, down_bias, gain_second, shift_second)
    shapes = [(3, D, D), (D,), (D,), (D, D), (D,), (D,), (D,), (D, FF), (FF,), (FF, D), (D,), (D,), (D,)]
    initial = tuple((jnp.zeros(shape_item, jnp.float32) for shape_item in shapes))

    def one_group(totals, block):
        token_block, segment_block, cot_block = block
        out_block, grad_block, grads = group_pass(token_block, segment_block, cot_block, weights)
        return (jax.tree.map(add_terms, totals, grads), (out_block, grad_block))
    blocks = (tokens.reshape(groups, CAP, D), segment_ids.reshape(groups, CAP), cotangent.reshape(groups, CAP, D))
    totals, outputs = lax.scan(one_group, initial, blocks)
    block_out = outputs[0].reshape(TOKENS, D)
    input_grad = outputs[1].reshape(TOKENS, D)
    return (block_out, input_grad, totals[0], totals[1], totals[2], totals[3], totals[4], totals[5], totals[6], totals[7], totals[8], totals[9], totals[10], totals[11], totals[12])
```

```python
import jax
import jax.numpy as jnp
from jax import lax
from jax.experimental import pallas as pl
from jax.experimental.pallas import tpu as pltpu
from jax.sharding import PartitionSpec as P

HD = 64
MESH = pl.DeviceIdType.MESH
VM = pl.BlockSpec(memory_space=pltpu.VMEM)
LIMIT = 60 * 1024 * 1024
TPIECES = 4
DPIECES = 4


EPSILON = 1e-05
TANH_SCALE = 0.7978845608028654
CUBIC = 0.044715


def norm_forward(values_in, norm_gain, norm_shift):
    row_mean = jnp.mean(values_in, axis=-1, keepdims=True)
    centered = values_in - row_mean
    inverse = lax.rsqrt(jnp.mean(centered * centered, axis=-1, keepdims=True) + EPSILON)
    normed = centered * inverse
    return (normed, inverse, normed * norm_gain + norm_shift)


def norm_backward(grad_out, normed, inverse, norm_gain):
    scaled = grad_out * norm_gain
    return inverse * (
        scaled
        - jnp.mean(scaled, axis=-1, keepdims=True)
        - normed * jnp.mean(scaled * normed, axis=-1, keepdims=True)
    )


def gelu_pair(pre_act):
    tangent = jnp.tanh(TANH_SCALE * (pre_act + CUBIC * pre_act * pre_act * pre_act))
    gelu_value = 0.5 * pre_act * (1.0 + tangent)
    gelu_slope = 0.5 * (1.0 + tangent) + 0.5 * pre_act * (1.0 - tangent * tangent) * TANH_SCALE * (
        1.0 + 3.0 * CUBIC * pre_act * pre_act
    )
    return (gelu_value, gelu_slope)


def contract_rows(left_mat, right_mat):
    return lax.dot_general(
        left_mat, right_mat, (((0,), (0,)), ((), ())), preferred_element_type=jnp.float32
    )


def contract_cols(left_mat, right_mat):
    return lax.dot_general(
        left_mat, right_mat, (((1,), (1,)), ((), ())), preferred_element_type=jnp.float32
    )


def allowed_mask(segments):
    position = jnp.arange(segments.shape[0])
    return (segments[:, None] == segments[None, :]) & (position[None, :] <= position[:, None])


def head_scores(queries, keys_bf, allowed):
    scaling = queries.shape[-1] ** (-0.5)
    scores = (
        jnp.einsum("qhd,khd->hqk", queries, keys_bf, preferred_element_type=jnp.float32) * scaling
    )
    return jnp.where(allowed[None], scores, -jnp.inf)


def attend(queries, keys_bf, values_bf, allowed):
    scores = head_scores(queries, keys_bf, allowed)
    top_score = jnp.max(scores, axis=-1, keepdims=True)
    log_sum = top_score + jnp.log(jnp.sum(jnp.exp(scores - top_score), axis=-1, keepdims=True))
    probs = jnp.exp(scores - log_sum).astype(jnp.bfloat16)
    mixed = jnp.einsum("hqk,khd->qhd", probs, values_bf, preferred_element_type=jnp.float32)
    return (mixed, log_sum)


def attend_back(queries, keys_bf, values_bf, allowed, log_sum, grad_mixed):
    probs_full = jnp.exp(head_scores(queries, keys_bf, allowed) - log_sum)
    probs_bf = probs_full.astype(jnp.bfloat16)
    grad_values = jnp.einsum(
        "hqk,qhd->khd", probs_bf, grad_mixed, preferred_element_type=jnp.float32
    )
    grad_probs = jnp.einsum(
        "qhd,khd->hqk", grad_mixed, values_bf, preferred_element_type=jnp.float32
    )
    scaling = queries.shape[-1] ** (-0.5)
    grad_scores = (
        probs_full
        * (grad_probs - jnp.sum(probs_full * grad_probs, axis=-1, keepdims=True))
        * scaling
    ).astype(jnp.bfloat16)
    grad_queries = jnp.einsum(
        "hqk,khd->qhd", grad_scores, keys_bf, preferred_element_type=jnp.float32
    )
    grad_keys = jnp.einsum("hqk,qhd->khd", grad_scores, queries, preferred_element_type=jnp.float32)
    return (grad_queries, grad_keys, grad_values)


def push(src, dst, send_sem, recv_sem, device):
    copy = pltpu.make_async_remote_copy(
        src_ref=src,
        dst_ref=dst,
        send_sem=send_sem,
        recv_sem=recv_sem,
        device_id=device,
        device_id_type=MESH,
    )
    copy.start()
    return copy


def tensor_scratch(count, rows, width):
    piece = rows // 2 // TPIECES
    buf = pltpu.VMEM((count * TPIECES, piece, width), jnp.float32)
    sem = pltpu.SemaphoreType.DMA((count * TPIECES,))
    return [buf] * 5 + [sem] * 6


class TensorSum:
    def __init__(self, parts, outs, scratch):
        self.parts, self.outs = parts, outs
        self.rx, self.mid, self.ry, self.fin, self.rb = scratch[:5]
        self.sems = scratch[5:11]
        dp = lax.axis_index("dp")
        me = lax.axis_index("tensor")
        low = me % 2
        self.near = (dp, me + 1 - 2 * low)
        self.far = (dp, me + 2 - 4 * (me // 2))
        half = parts[0].shape[0] // 2
        self.piece = half // TPIECES
        self.mine, self.other = low * half, (1 - low) * half
        self.units = [(a, k) for a in range(len(parts)) for k in range(TPIECES)]
        self.copies = [[], [], []]

    def peers(self):
        return [self.near, self.far]

    def window(self, base, k):
        return pl.ds(pl.multiple_of(base + k * self.piece, 8), self.piece)

    def send_halves(self):
        for u, (a, k) in enumerate(self.units):
            src = self.parts[a].at[self.window(self.other, k)]
            self.copies[0].append(
                push(src, self.rx.at[u], self.sems[0].at[u], self.sems[1].at[u], self.near)
            )

    def cross(self, u):
        a, k = self.units[u]
        self.copies[0][u].wait_recv()
        self.mid[u] = self.parts[a][self.window(self.mine, k)] + self.rx[u]
        self.copies[1].append(
            push(self.mid.at[u], self.ry.at[u], self.sems[2].at[u], self.sems[3].at[u], self.far)
        )

    def finish(self, u):
        a, k = self.units[u]
        self.copies[1][u].wait_recv()
        total = self.mid[u] + self.ry[u]
        self.fin[u] = total
        self.outs[a][self.window(self.mine, k)] = total
        self.copies[2].append(
            push(self.fin.at[u], self.rb.at[u], self.sems[4].at[u], self.sems[5].at[u], self.near)
        )

    def collect(self, u):
        a, k = self.units[u]
        self.copies[2][u].wait_recv()
        self.outs[a][self.window(self.other, k)] = self.rb[u]

    def drain(self):
        for group in self.copies:
            for copy in group:
                copy.wait_send()


def greet(peers):
    barrier = pltpu.get_barrier_semaphore()
    for peer in peers:
        pl.semaphore_signal(barrier, inc=1, device_id=peer, device_id_type=MESH)
    pl.semaphore_wait(barrier, len(peers))


def tensor_kernel(count, *refs):
    parts, outs, scratch = refs[:count], refs[count : 2 * count], refs[2 * count :]
    job = TensorSum(parts, outs, scratch)
    greet(job.peers())
    job.send_halves()
    for u in range(len(job.units)):
        job.cross(u)
    for u in range(len(job.units)):
        job.finish(u)
    for u in range(len(job.units)):
        job.collect(u)
    job.drain()


def tensor_sum(parts, number):
    rows, width = parts[0].shape
    if lax.axis_size("tensor") != 4:
        return lax.psum(parts, "tensor")
    return pl.pallas_call(
        lambda *refs: tensor_kernel(len(parts), *refs),
        out_shape=[jax.ShapeDtypeStruct((rows, width), jnp.float32)] * len(parts),
        in_specs=[VM] * len(parts),
        out_specs=[VM] * len(parts),
        scratch_shapes=tensor_scratch(len(parts), rows, width),
        compiler_params=pltpu.CompilerParams(
            collective_id=number, has_side_effects=True, vmem_limit_bytes=LIMIT
        ),
        name="tensor_sum",
    )(*parts)


def final_kernel(nt, nd, *refs):
    refs = list(refs)
    parts, mats, (normed, small) = refs[:nt], refs[nt : nt + nd], refs[nt + nd : nt + nd + 2]
    refs = refs[nt + nd + 2 :]
    part_outs, mat_outs, small_out = refs[:nt], refs[nt : nt + nd], refs[nt + nd]
    refs = refs[nt + nd + 1 :]
    job = TensorSum(parts, part_outs, refs[:11])
    rx, own, rz, mid, ry, fin, re, rg = refs[11:19]
    sx, qx, sz, qz, sy, qy, se, qe, sg, qg = refs[19:29]
    slots, mine_small, ss, qs = refs[29:33]

    dp = lax.axis_index("dp")
    me = lax.axis_index("tensor")
    column, line = dp % 2, dp // 2
    inner = (line == 1) | (line == 2)
    edge = (line == 0) | (line == 3)
    across = (dp + 1 - 2 * column, me)
    upper = line // 2
    odd = line % 2
    beside = ((line + 1 - 2 * odd) * 2 + column, me)
    middle = ((1 - upper + 1) * 2 + column, me)
    peers = [((dp + j) % 8, me) for j in range(1, 8)]
    half = mats[0].shape[0] // 2
    piece = half // DPIECES
    units = [(a, k) for a in range(nd) for k in range(DPIECES)]
    count = len(units)

    def window(index, k):
        return pl.ds(pl.multiple_of(index * half + k * piece, 8), piece)

    def remote(src, dst, send, recv, device):
        return pltpu.make_async_remote_copy(
            src_ref=src,
            dst_ref=dst,
            send_sem=send,
            recv_sem=recv,
            device_id=device,
            device_id_type=MESH,
        )

    def to_across(u):
        a, k = units[u]
        src = mats[a].at[window(1 - column, k)]
        return remote(src, rx.at[u], sx.at[u], qx.at[u], across)

    def to_middle_side(u):
        return remote(own.at[u], rz.at[u], sz.at[u], qz.at[u], beside)

    def between_middles(u):
        return remote(mid.at[u], ry.at[u], sy.at[u], qy.at[u], middle)

    def to_edge(u):
        return remote(fin.at[u], re.at[u], se.at[u], qe.at[u], beside)

    def give_back(u, src):
        return remote(src.at[u], rg.at[u], sg.at[u], qg.at[u], across)

    def stage_a(u):
        a, k = units[u]
        to_across(u).wait_recv()
        own[u] = mats[a][window(column, k)] + rx[u]

        @pl.when(edge)
        def _():
            to_middle_side(u).start()

    def stage_b(u):
        @pl.when(inner)
        def _():
            to_middle_side(u).wait_recv()
            mid[u] = own[u] + rz[u]
            between_middles(u).start()

    def stage_c(u):
        a, k = units[u]

        @pl.when(inner)
        def _():
            between_middles(u).wait_recv()
            total = mid[u] + ry[u]
            fin[u] = total
            to_edge(u).start()
            give_back(u, fin).start()
            mat_outs[a][window(column, k)] = total

    def stage_d(u):
        a, k = units[u]

        @pl.when(edge)
        def _():
            to_edge(u).wait_recv()
            give_back(u, re).start()
            mat_outs[a][window(column, k)] = re[u]

    def stage_e(u):
        a, k = units[u]
        give_back(u, fin).wait_recv()
        mat_outs[a][window(1 - column, k)] = rg[u]

    greet(peers + job.peers())
    job.send_halves()
    for u in range(count):
        to_across(u).start()
    for u in range(len(job.units)):
        job.cross(u)
    pending = list(range(len(job.units)))
    stages = [stage_a, stage_b, stage_c, stage_d]
    for step in range(count + len(stages) - 1):
        for lag, stage in enumerate(stages):
            if 0 <= step - lag < count:
                stage(step - lag)
        for _ in range(2):
            if pending:
                job.finish(pending.pop(0))
    for u in pending:
        job.finish(u)
    for u in range(len(job.units)):
        job.collect(u)

    summed = part_outs[0][...]
    row = lax.broadcasted_iota(jnp.int32, small.shape, 0)
    gain = jnp.sum(summed * normed[...], axis=0, keepdims=True)
    shift = jnp.sum(summed, axis=0, keepdims=True)
    mine_small[...] = jnp.where(row == 0, gain, jnp.where(row == 1, shift, small[...]))
    slots[dp] = mine_small[...]
    notes = []
    for j, peer in enumerate(peers):
        notes.append(push(mine_small, slots.at[dp], ss.at[j], qs.at[j], peer))
    for u in range(count):
        stage_e(u)
    for note in notes:
        note.wait_recv()
    total = slots[0]
    for j in range(1, 8):
        total = total + slots[j]
    small_out[...] = total

    job.drain()
    for note in notes:
        note.wait_send()
    for u in range(count):
        to_across(u).wait_send()
        give_back(u, fin).wait_send()

    @pl.when(edge)
    def _():
        for u in range(count):
            to_middle_side(u).wait_send()

    @pl.when(inner)
    def _():
        for u in range(count):
            between_middles(u).wait_send()
            to_edge(u).wait_send()


def final_sums(parts, mats, normed, small, number):
    nt, nd = len(parts), len(mats)
    if lax.axis_size("tensor") != 4 or lax.axis_size("dp") != 8:
        parts = tensor_sum(parts, number)
        gain = jnp.sum(parts[0] * normed, axis=0)
        small = small.at[0].set(gain).at[1].set(jnp.sum(parts[0], axis=0))
        mats, small = lax.psum((mats, small), "dp")
        return (parts, mats, small)
    rows, width = mats[0].shape
    count = nd * DPIECES
    buf = pltpu.VMEM((count, rows // 2 // DPIECES, width), jnp.float32)
    sem = pltpu.SemaphoreType.DMA((count,))
    out = pl.pallas_call(
        lambda *refs: final_kernel(nt, nd, *refs),
        out_shape=[jax.ShapeDtypeStruct(p.shape, jnp.float32) for p in (*parts, *mats, small)],
        in_specs=[VM] * (nt + nd + 2),
        out_specs=[VM] * (nt + nd + 1),
        scratch_shapes=tensor_scratch(nt, *parts[0].shape)
        + [buf] * 8
        + [sem] * 10
        + [
            pltpu.VMEM((8, *small.shape), jnp.float32),
            pltpu.VMEM(small.shape, jnp.float32),
            pltpu.SemaphoreType.DMA((7,)),
            pltpu.SemaphoreType.DMA((7,)),
        ],
        compiler_params=pltpu.CompilerParams(
            collective_id=number, has_side_effects=True, vmem_limit_bytes=LIMIT
        ),
        name="final_sums",
    )(*parts, *mats, normed, small)
    return (out[:nt], out[nt : nt + nd], out[nt + nd])


def shards(
    tokens,
    segment_ids,
    cotangent,
    attn_input,
    query_bias,
    value_bias,
    attn_output,
    output_bias,
    gain_first,
    shift_first,
    hidden_weight,
    hidden_bias,
    down_weight,
    down_bias,
    gain_second,
    shift_second,
):
    row_count = tokens.shape[0]
    local_width = attn_input.shape[2]
    valid = (segment_ids >= 0)[:, None]
    cot_masked = jnp.where(valid, cotangent, jnp.zeros_like(cotangent))
    allowed = allowed_mask(segment_ids)
    resid_in = tokens.astype(jnp.float32)
    normed_one, inverse_one, pre_one = norm_forward(resid_in, gain_first, shift_first)
    hidden_one = pre_one.astype(jnp.bfloat16)
    projected = jnp.einsum(
        "rd,tdc->trc", hidden_one, attn_input, preferred_element_type=jnp.float32
    )
    queries = (projected[0] + query_bias).astype(jnp.bfloat16).reshape(row_count, -1, HD)
    keys_bf = projected[1].astype(jnp.bfloat16).reshape(row_count, -1, HD)
    values_bf = (projected[2] + value_bias).astype(jnp.bfloat16).reshape(row_count, -1, HD)
    mixed, log_sum = attend(queries, keys_bf, values_bf, allowed)
    attended = mixed.reshape(row_count, local_width).astype(jnp.bfloat16)
    attn_part = jnp.dot(attended, attn_output, preferred_element_type=jnp.float32)
    middle = resid_in + tensor_sum([attn_part], 0)[0] + output_bias
    normed_two, inverse_two, pre_two = norm_forward(middle, gain_second, shift_second)
    hidden_two = pre_two.astype(jnp.bfloat16)
    pre_act = jnp.dot(hidden_two, hidden_weight, preferred_element_type=jnp.float32) + hidden_bias
    gelu_value, gelu_slope = gelu_pair(pre_act)
    activation = gelu_value.astype(jnp.bfloat16)
    mlp_part = jnp.dot(activation, down_weight, preferred_element_type=jnp.float32)
    grad_top = cot_masked.astype(jnp.float32)
    grad_down_bias = jnp.sum(grad_top, axis=0)
    grad_down_weight = contract_rows(activation, cot_masked)
    grad_pre = contract_cols(cot_masked, down_weight) * gelu_slope
    grad_hidden_bias = jnp.sum(grad_pre, axis=0)
    grad_pre_bf = grad_pre.astype(jnp.bfloat16)
    grad_hidden_weight = contract_rows(hidden_two, grad_pre_bf)
    two_part = contract_cols(grad_pre_bf, hidden_weight)
    two_part, grad_hidden_weight, grad_down_weight = lax.optimization_barrier(
        (two_part, grad_hidden_weight, grad_down_weight)
    )
    grad_hidden_weight, grad_down_weight = lax.psum((grad_hidden_weight, grad_down_weight), "dp")
    grad_two = tensor_sum([two_part], 1)[0]
    grad_gain_second = jnp.sum(grad_two * normed_two, axis=0)
    grad_shift_second = jnp.sum(grad_two, axis=0)
    grad_middle = grad_top + norm_backward(grad_two, normed_two, inverse_two, gain_second)
    grad_output_bias = jnp.sum(grad_middle, axis=0)
    grad_middle_bf = grad_middle.astype(jnp.bfloat16)
    output_grad = contract_rows(grad_middle_bf, attended)
    grad_attended = (
        contract_cols(grad_middle_bf, attn_output).astype(jnp.bfloat16).reshape(row_count, -1, HD)
    )
    grad_queries, grad_keys, grad_values = attend_back(
        queries, keys_bf, values_bf, allowed, log_sum, grad_attended
    )
    grad_queries = grad_queries.reshape(row_count, local_width)
    grad_keys = grad_keys.reshape(row_count, local_width)
    grad_values = grad_values.reshape(row_count, local_width)
    grad_query_bias = jnp.sum(grad_queries, axis=0)
    grad_value_bias = jnp.sum(grad_values, axis=0)
    grad_flat = jnp.concatenate([grad_queries, grad_keys, grad_values], axis=1).astype(jnp.bfloat16)
    stack_grad = contract_rows(hidden_one, grad_flat)
    attn_mat = jnp.concatenate([stack_grad, output_grad], axis=1)
    attn_flat = jnp.concatenate([attn_input[0], attn_input[1], attn_input[2]], axis=1)
    one_part = contract_cols(grad_flat, attn_flat)
    width = tokens.shape[1]
    zeros = jnp.zeros((2 * width,), jnp.float32)
    pieces = [
        zeros,
        grad_output_bias,
        grad_hidden_bias,
        grad_down_bias,
        grad_gain_second,
        grad_shift_second,
        grad_query_bias,
        grad_value_bias,
    ]
    flat = jnp.concatenate(pieces)
    rows = -(-flat.shape[0] // (8 * width)) * 8
    small = jnp.pad(flat, (0, rows * width - flat.shape[0])).reshape(rows, width)
    (grad_one, mlp_sum), (attn_mat,), small = final_sums(
        [one_part, mlp_part], [attn_mat], normed_one, small, 2
    )
    input_grad = (
        grad_middle + norm_backward(grad_one, normed_one, inverse_one, gain_first)
    ).astype(jnp.bfloat16)
    out_full = middle + mlp_sum + down_bias
    block_out = jnp.where(valid, out_full, jnp.zeros_like(out_full)).astype(jnp.bfloat16)
    grad_attn_input = jnp.stack(
        [attn_mat[:, m * local_width : (m + 1) * local_width] for m in range(3)]
    )
    grad_attn_output = attn_mat[:, 3 * local_width :].T
    flat = small.reshape(-1)
    grad_gain_first, grad_shift_first = flat[:width], flat[width : 2 * width]
    values, start = [], 2 * width
    for item in pieces[1:]:
        values.append(flat[start : start + item.shape[0]])
        start += item.shape[0]
    (
        grad_output_bias,
        grad_hidden_bias,
        grad_down_bias,
        grad_gain_second,
        grad_shift_second,
        grad_query_bias,
        grad_value_bias,
    ) = values
    return (
        block_out,
        input_grad,
        grad_attn_input,
        grad_query_bias,
        grad_value_bias,
        grad_attn_output,
        grad_output_bias,
        grad_gain_first,
        grad_shift_first,
        grad_hidden_weight,
        grad_hidden_bias,
        grad_down_weight,
        grad_down_bias,
        grad_gain_second,
        grad_shift_second,
    )


def solution(mesh):
    return jax.shard_map(
        shards,
        mesh=mesh,
        in_specs=(
            P("dp", None),
            P("dp"),
            P("dp", None),
            P(None, None, "tensor"),
            P("tensor"),
            P("tensor"),
            P("tensor", None),
            P(),
            P(),
            P(),
            P(None, "tensor"),
            P("tensor"),
            P("tensor", None),
            P(),
            P(),
            P(),
        ),
        out_specs=(
            P("dp", None),
            P("dp", None),
            P(None, None, "tensor"),
            P("tensor"),
            P("tensor"),
            P("tensor", None),
            P(),
            P(),
            P(),
            P(None, "tensor"),
            P("tensor"),
            P("tensor", None),
            P(),
            P(),
            P(),
        ),
        check_vma=False,
    )
```

```python
import jax
import jax.numpy as jnp
from jax import lax
from jax.experimental import pallas as pl
from jax.experimental.pallas import tpu as pltpu
from jax.sharding import PartitionSpec as P

HD = 64
MESH = pl.DeviceIdType.MESH
VM = pl.BlockSpec(memory_space=pltpu.VMEM)
LIMIT = 60 * 1024 * 1024
TPIECES = 4
DPIECES = 4


EPSILON = 1e-05
TANH_SCALE = 0.7978845608028654
CUBIC = 0.044715


def norm_forward(values_in, norm_gain, norm_shift):
    row_mean = jnp.mean(values_in, axis=-1, keepdims=True)
    centered = values_in - row_mean
    inverse = lax.rsqrt(jnp.mean(centered * centered, axis=-1, keepdims=True) + EPSILON)
    normed = centered * inverse
    return (normed, inverse, normed * norm_gain + norm_shift)


def norm_backward(grad_out, normed, inverse, norm_gain):
    scaled = grad_out * norm_gain
    return inverse * (
        scaled
        - jnp.mean(scaled, axis=-1, keepdims=True)
        - normed * jnp.mean(scaled * normed, axis=-1, keepdims=True)
    )


def gelu_pair(pre_act):
    tangent = jnp.tanh(TANH_SCALE * (pre_act + CUBIC * pre_act * pre_act * pre_act))
    gelu_value = 0.5 * pre_act * (1.0 + tangent)
    gelu_slope = 0.5 * (1.0 + tangent) + 0.5 * pre_act * (1.0 - tangent * tangent) * TANH_SCALE * (
        1.0 + 3.0 * CUBIC * pre_act * pre_act
    )
    return (gelu_value, gelu_slope)


def contract_rows(left_mat, right_mat):
    return lax.dot_general(
        left_mat, right_mat, (((0,), (0,)), ((), ())), preferred_element_type=jnp.float32
    )


def contract_cols(left_mat, right_mat):
    return lax.dot_general(
        left_mat, right_mat, (((1,), (1,)), ((), ())), preferred_element_type=jnp.float32
    )


def allowed_mask(segments):
    position = jnp.arange(segments.shape[0])
    return (segments[:, None] == segments[None, :]) & (position[None, :] <= position[:, None])


def head_scores(queries, keys_bf, allowed):
    scaling = queries.shape[-1] ** (-0.5)
    scores = (
        jnp.einsum("qhd,khd->hqk", queries, keys_bf, preferred_element_type=jnp.float32) * scaling
    )
    return jnp.where(allowed[None], scores, -jnp.inf)


def attend(queries, keys_bf, values_bf, allowed):
    scores = head_scores(queries, keys_bf, allowed)
    top_score = jnp.max(scores, axis=-1, keepdims=True)
    log_sum = top_score + jnp.log(jnp.sum(jnp.exp(scores - top_score), axis=-1, keepdims=True))
    probs = jnp.exp(scores - log_sum).astype(jnp.bfloat16)
    mixed = jnp.einsum("hqk,khd->qhd", probs, values_bf, preferred_element_type=jnp.float32)
    return (mixed, log_sum)


def attend_back(queries, keys_bf, values_bf, allowed, log_sum, grad_mixed):
    probs_full = jnp.exp(head_scores(queries, keys_bf, allowed) - log_sum)
    probs_bf = probs_full.astype(jnp.bfloat16)
    grad_values = jnp.einsum(
        "hqk,qhd->khd", probs_bf, grad_mixed, preferred_element_type=jnp.float32
    )
    grad_probs = jnp.einsum(
        "qhd,khd->hqk", grad_mixed, values_bf, preferred_element_type=jnp.float32
    )
    scaling = queries.shape[-1] ** (-0.5)
    grad_scores = (
        probs_full
        * (grad_probs - jnp.sum(probs_full * grad_probs, axis=-1, keepdims=True))
        * scaling
    ).astype(jnp.bfloat16)
    grad_queries = jnp.einsum(
        "hqk,khd->qhd", grad_scores, keys_bf, preferred_element_type=jnp.float32
    )
    grad_keys = jnp.einsum("hqk,qhd->khd", grad_scores, queries, preferred_element_type=jnp.float32)
    return (grad_queries, grad_keys, grad_values)


def push(src, dst, send_sem, recv_sem, device):
    copy = pltpu.make_async_remote_copy(
        src_ref=src,
        dst_ref=dst,
        send_sem=send_sem,
        recv_sem=recv_sem,
        device_id=device,
        device_id_type=MESH,
    )
    copy.start()
    return copy


def tensor_scratch(count, rows, width):
    piece = rows // 2 // TPIECES
    buf = pltpu.VMEM((count * TPIECES, piece, width), jnp.float32)
    sem = pltpu.SemaphoreType.DMA((count * TPIECES,))
    return [buf] * 5 + [sem] * 6


class TensorSum:
    def __init__(self, parts, outs, scratch):
        self.parts, self.outs = parts, outs
        self.rx, self.mid, self.ry, self.fin, self.rb = scratch[:5]
        self.sems = scratch[5:11]
        dp = lax.axis_index("dp")
        me = lax.axis_index("tensor")
        low = me % 2
        self.near = (dp, me + 1 - 2 * low)
        self.far = (dp, me + 2 - 4 * (me // 2))
        half = parts[0].shape[0] // 2
        self.piece = half // TPIECES
        self.mine, self.other = low * half, (1 - low) * half
        self.units = [(a, k) for a in range(len(parts)) for k in range(TPIECES)]
        self.copies = [[], [], []]

    def peers(self):
        return [self.near, self.far]

    def window(self, base, k):
        return pl.ds(pl.multiple_of(base + k * self.piece, 8), self.piece)

    def send_halves(self):
        for u, (a, k) in enumerate(self.units):
            src = self.parts[a].at[self.window(self.other, k)]
            self.copies[0].append(
                push(src, self.rx.at[u], self.sems[0].at[u], self.sems[1].at[u], self.near)
            )

    def cross(self, u):
        a, k = self.units[u]
        self.copies[0][u].wait_recv()
        self.mid[u] = self.parts[a][self.window(self.mine, k)] + self.rx[u]
        self.copies[1].append(
            push(self.mid.at[u], self.ry.at[u], self.sems[2].at[u], self.sems[3].at[u], self.far)
        )

    def finish(self, u):
        a, k = self.units[u]
        self.copies[1][u].wait_recv()
        total = self.mid[u] + self.ry[u]
        self.fin[u] = total
        self.outs[a][self.window(self.mine, k)] = total
        self.copies[2].append(
            push(self.fin.at[u], self.rb.at[u], self.sems[4].at[u], self.sems[5].at[u], self.near)
        )

    def collect(self, u):
        a, k = self.units[u]
        self.copies[2][u].wait_recv()
        self.outs[a][self.window(self.other, k)] = self.rb[u]

    def drain(self):
        for group in self.copies:
            for copy in group:
                copy.wait_send()


def greet(peers):
    barrier = pltpu.get_barrier_semaphore()
    for peer in peers:
        pl.semaphore_signal(barrier, inc=1, device_id=peer, device_id_type=MESH)
    pl.semaphore_wait(barrier, len(peers))


def tensor_kernel(count, *refs):
    parts, outs, scratch = refs[:count], refs[count : 2 * count], refs[2 * count :]
    job = TensorSum(parts, outs, scratch)
    greet(job.peers())
    job.send_halves()
    for u in range(len(job.units)):
        job.cross(u)
    for u in range(len(job.units)):
        job.finish(u)
    for u in range(len(job.units)):
        job.collect(u)
    job.drain()


def tensor_sum(parts, number):
    rows, width = parts[0].shape
    if lax.axis_size("tensor") != 4:
        return lax.psum(parts, "tensor")
    return pl.pallas_call(
        lambda *refs: tensor_kernel(len(parts), *refs),
        out_shape=[jax.ShapeDtypeStruct((rows, width), jnp.float32)] * len(parts),
        in_specs=[VM] * len(parts),
        out_specs=[VM] * len(parts),
        scratch_shapes=tensor_scratch(len(parts), rows, width),
        compiler_params=pltpu.CompilerParams(
            collective_id=number, has_side_effects=True, vmem_limit_bytes=LIMIT
        ),
        name="tensor_sum",
    )(*parts)


def dot(left, right, left_dim, right_dim):
    return lax.dot_general(
        left, right, (((left_dim,), (right_dim,)), ((), ())), preferred_element_type=jnp.float32
    )


def backward_kernel(heads, *refs):
    (two_part, mlp_part, down_mat, hidden_mat, middle, tokens, cot, hidden_one, queries, keys, values) = refs[:11]
    (attended, attn_output, attn_rows, seg_col, seg_row, vectors) = refs[11:17]
    block_out, input_grad, down_out, hidden_out, attn_out, small_out = refs[17:23]
    two_sum, mlp_sum, one_part, one_sum, attn_mat, grad_middle = refs[23:29]
    job_two = TensorSum([two_part], [two_sum], refs[29:40])
    job_mlp = TensorSum([mlp_part], [mlp_sum], refs[40:51])
    job_one = TensorSum([one_part], [one_sum], refs[51:62])
    rx, own, rz, ry, rg = refs[62:67]
    sx, qx, sz, qz, sy, qy, sg, qg = refs[67:75]
    slots, mine_small, ss, qs = refs[75:79]
    mats, outs = [down_mat, hidden_mat, attn_mat], [down_out, hidden_out, attn_out]

    dp = lax.axis_index("dp")
    me = lax.axis_index("tensor")
    column, line = dp % 2, dp // 2
    inner = (line == 1) | (line == 2)
    edge = (line == 0) | (line == 3)
    across = (dp + 1 - 2 * column, me)
    odd = line % 2
    beside = ((line + 1 - 2 * odd) * 2 + column, me)
    middle_peer = ((2 - line // 2) * 2 + column, me)
    peers = [((dp + j) % 8, me) for j in range(1, 8)]
    half = down_mat.shape[0] // 2
    piece = half // DPIECES
    units = [(m, k) for m in range(3) for k in range(DPIECES)]
    count = len(units)

    def window(index, k):
        return pl.ds(pl.multiple_of(index * half + k * piece, 8), piece)

    def remote(src, dst, send, recv, device):
        return pltpu.make_async_remote_copy(
            src_ref=src,
            dst_ref=dst,
            send_sem=send,
            recv_sem=recv,
            device_id=device,
            device_id_type=MESH,
        )

    def to_across(u):
        m, k = units[u]
        src = mats[m].at[window(1 - column, k)]
        return remote(src, rx.at[u], sx.at[u], qx.at[u], across)

    def to_beside(u, src):
        return remote(src, rz.at[u], sz.at[u], qz.at[u], beside)

    def between_middles(u):
        return remote(own.at[u], ry.at[u], sy.at[u], qy.at[u], middle_peer)

    def give_back(u, src):
        return remote(src, rg.at[u], sg.at[u], qg.at[u], across)

    def done(u):
        m, k = units[u]
        return outs[m].at[window(column, k)]

    def stage_a(u):
        m, k = units[u]
        to_across(u).wait_recv()
        own[u] = mats[m][window(column, k)] + rx[u]

        @pl.when(edge)
        def _():
            to_beside(u, own.at[u]).start()

    def stage_b(u):
        @pl.when(inner)
        def _():
            to_beside(u, own.at[u]).wait_recv()
            own[u] = own[u] + rz[u]
            between_middles(u).start()

    def stage_c(u):
        m, k = units[u]

        @pl.when(inner)
        def _():
            between_middles(u).wait_recv()
            outs[m][window(column, k)] = own[u] + ry[u]
            to_beside(u, done(u)).start()
            give_back(u, done(u)).start()

    def stage_d(u):
        m, k = units[u]

        @pl.when(edge)
        def _():
            to_beside(u, own.at[u]).wait_recv()
            give_back(u, rz.at[u]).start()
            outs[m][window(column, k)] = rz[u]

    def stage_e(u):
        m, k = units[u]
        give_back(u, own.at[u]).wait_recv()
        outs[m][window(1 - column, k)] = rg[u]

    stages = [stage_a, stage_b, stage_c, stage_d]

    def step(at):
        for lag, stage in enumerate(stages):
            if 0 <= at - lag < count:
                stage(at - lag)

    def each(call, job):
        for u in range(len(job.units)):
            call(u)

    greet(peers + job_two.peers())
    job_two.send_halves()
    job_mlp.send_halves()
    for u in range(2 * DPIECES):
        to_across(u).start()
    each(job_two.cross, job_two)
    each(job_mlp.cross, job_mlp)
    each(job_two.finish, job_two)
    each(job_two.collect, job_two)

    gain_first, gain_second, down_bias = vectors[0:1, :], vectors[1:2, :], vectors[2:3, :]
    normed_two, inverse_two, _ = norm_forward(middle[...], gain_second, 0.0)
    grad_two = two_sum[...]
    mine_small[...] = jnp.zeros_like(mine_small)
    mine_small[0:2, :] = vectors[3:5, :]
    mine_small[2:3, :] = jnp.sum(grad_two * normed_two, axis=0, keepdims=True)
    mine_small[3:4, :] = jnp.sum(grad_two, axis=0, keepdims=True)
    grad_mid = cot[...].astype(jnp.float32) + norm_backward(
        grad_two, normed_two, inverse_two, gain_second
    )
    grad_middle[...] = grad_mid
    mine_small[4:5, :] = jnp.sum(grad_mid, axis=0, keepdims=True)
    mid_bf = grad_mid.astype(jnp.bfloat16)
    row_count, local_width = attended.shape
    attn_mat[3 * local_width :, :] = dot(attended[...], mid_bf, 0, 0)
    step(0)
    step(1)

    row_at = lax.broadcasted_iota(jnp.int32, (row_count, row_count), 0)
    col_at = lax.broadcasted_iota(jnp.int32, (row_count, row_count), 1)
    allowed = (seg_col[...] == seg_row[...]) & (col_at <= row_at)
    scaling = HD ** (-0.5)
    normal = hidden_one[...]
    for h in range(heads):
        query, key, value = queries[h], keys[h], values[h]
        scores = jnp.where(allowed, dot(query, key, 1, 1) * scaling, -jnp.inf)
        top = jnp.max(scores, axis=-1, keepdims=True)
        log_sum = top + jnp.log(jnp.sum(jnp.exp(scores - top), axis=-1, keepdims=True))
        probs = jnp.exp(scores - log_sum)
        grad_mixed = dot(mid_bf, attn_output[h * HD : (h + 1) * HD, :], 1, 1).astype(jnp.bfloat16)
        grad_value = dot(probs.astype(jnp.bfloat16), grad_mixed, 0, 0)
        grad_probs = dot(grad_mixed, value, 1, 1)
        weighted = jnp.sum(probs * grad_probs, axis=-1, keepdims=True)
        grad_scores = (probs * (grad_probs - weighted) * scaling).astype(jnp.bfloat16)
        grad_query = dot(grad_scores, key, 1, 0)
        grad_key = dot(grad_scores, query, 0, 0)
        mine_small[8 + h : 9 + h, 0:HD] = jnp.sum(grad_query, axis=0, keepdims=True)
        mine_small[8 + heads + h : 9 + heads + h, 0:HD] = jnp.sum(grad_value, axis=0, keepdims=True)
        for m, item in enumerate((grad_query, grad_key, grad_value)):
            item = item.astype(jnp.bfloat16)
            start = m * local_width + h * HD
            attn_mat[start : start + HD, :] = dot(item, normal, 0, 0)
            term = dot(item, attn_rows[start : start + HD, :], 1, 0)
            if h == 0 and m == 0:
                one_part[...] = term
            else:
                one_part[...] += term
        if h < heads - 1:
            step(2 + h)
    for u in range(2 * DPIECES, count):
        to_across(u).start()
    job_one.send_halves()
    at = 1 + heads
    step(at)
    each(job_one.cross, job_one)
    each(job_mlp.finish, job_mlp)
    step(at + 1)
    each(job_one.finish, job_one)
    each(job_mlp.collect, job_mlp)
    valid = seg_col[...] >= 0
    full = middle[...] + mlp_sum[...] + down_bias
    block_out[...] = jnp.where(valid, full, 0.0).astype(block_out.dtype)
    step(at + 2)
    each(job_one.collect, job_one)
    normed_one, inverse_one, _ = norm_forward(tokens[...].astype(jnp.float32), gain_first, 0.0)
    grad_one = one_sum[...]
    mine_small[5:6, :] = jnp.sum(grad_one * normed_one, axis=0, keepdims=True)
    mine_small[6:7, :] = jnp.sum(grad_one, axis=0, keepdims=True)
    slots[dp] = mine_small[...]
    notes = []
    for j, peer in enumerate(peers):
        notes.append(push(mine_small, slots.at[dp], ss.at[j], qs.at[j], peer))
    step(at + 3)
    back = norm_backward(grad_one, normed_one, inverse_one, gain_first)
    input_grad[...] = (grad_middle[...] + back).astype(input_grad.dtype)
    for i in range(at + 4, count + len(stages) - 1):
        step(i)
    for note in notes:
        note.wait_recv()
    total = slots[0]
    for j in range(1, 8):
        total = total + slots[j]
    small_out[...] = total
    for u in range(count):
        stage_e(u)

    for job in (job_two, job_mlp, job_one):
        job.drain()
    for note in notes:
        note.wait_send()
    for u in range(count):
        to_across(u).wait_send()
        to_beside(u, own.at[u]).wait_send()
        give_back(u, own.at[u]).wait_send()

    @pl.when(inner)
    def _():
        for u in range(count):
            between_middles(u).wait_send()


def backward_pass(operands, heads, number):
    rows, width = operands[0].shape
    square = jax.ShapeDtypeStruct((width, width), jnp.float32)
    small = (16, width)
    whole = pltpu.VMEM((rows, width), jnp.float32)
    count = 3 * DPIECES
    buf = pltpu.VMEM((count, width // 2 // DPIECES, width), jnp.float32)
    sem = pltpu.SemaphoreType.DMA((count,))
    tile = jax.ShapeDtypeStruct((rows, width), jnp.bfloat16)
    return pl.pallas_call(
        lambda *refs: backward_kernel(heads, *refs),
        out_shape=[tile, tile, square, square, square, jax.ShapeDtypeStruct(small, jnp.float32)],
        in_specs=[VM] * len(operands),
        out_specs=[VM] * 6,
        scratch_shapes=[whole] * 4
        + [pltpu.VMEM((width, width), jnp.float32), whole]
        + tensor_scratch(1, rows, width) * 3
        + [buf] * 5
        + [sem] * 8
        + [
            pltpu.VMEM((8, *small), jnp.float32),
            pltpu.VMEM(small, jnp.float32),
            pltpu.SemaphoreType.DMA((7,)),
            pltpu.SemaphoreType.DMA((7,)),
        ],
        compiler_params=pltpu.CompilerParams(
            collective_id=number, has_side_effects=True, vmem_limit_bytes=67043328
        ),
        name="backward_pass",
    )(*operands)


def plain_shards(
    tokens,
    segment_ids,
    cotangent,
    attn_input,
    query_bias,
    value_bias,
    attn_output,
    output_bias,
    gain_first,
    shift_first,
    hidden_weight,
    hidden_bias,
    down_weight,
    down_bias,
    gain_second,
    shift_second,
):
    row_count = tokens.shape[0]
    local_width = attn_input.shape[2]
    valid = (segment_ids >= 0)[:, None]
    cot_masked = jnp.where(valid, cotangent, jnp.zeros_like(cotangent))
    allowed = allowed_mask(segment_ids)
    resid_in = tokens.astype(jnp.float32)
    normed_one, inverse_one, pre_one = norm_forward(resid_in, gain_first, shift_first)
    hidden_one = pre_one.astype(jnp.bfloat16)
    projected = jnp.einsum(
        "rd,tdc->trc", hidden_one, attn_input, preferred_element_type=jnp.float32
    )
    queries = (projected[0] + query_bias).astype(jnp.bfloat16).reshape(row_count, -1, HD)
    keys_bf = projected[1].astype(jnp.bfloat16).reshape(row_count, -1, HD)
    values_bf = (projected[2] + value_bias).astype(jnp.bfloat16).reshape(row_count, -1, HD)
    mixed, log_sum = attend(queries, keys_bf, values_bf, allowed)
    attended = mixed.reshape(row_count, local_width).astype(jnp.bfloat16)
    attn_part = jnp.dot(attended, attn_output, preferred_element_type=jnp.float32)
    middle = resid_in + lax.psum(attn_part, "tensor") + output_bias
    normed_two, inverse_two, pre_two = norm_forward(middle, gain_second, shift_second)
    hidden_two = pre_two.astype(jnp.bfloat16)
    pre_act = jnp.dot(hidden_two, hidden_weight, preferred_element_type=jnp.float32) + hidden_bias
    gelu_value, gelu_slope = gelu_pair(pre_act)
    activation = gelu_value.astype(jnp.bfloat16)
    mlp_part = jnp.dot(activation, down_weight, preferred_element_type=jnp.float32)
    out_full = middle + lax.psum(mlp_part, "tensor") + down_bias
    block_out = jnp.where(valid, out_full, jnp.zeros_like(out_full)).astype(jnp.bfloat16)
    grad_top = cot_masked.astype(jnp.float32)
    grad_down_bias = jnp.sum(grad_top, axis=0)
    grad_down_weight = contract_rows(activation, cot_masked)
    grad_pre = contract_cols(cot_masked, down_weight) * gelu_slope
    grad_hidden_bias = jnp.sum(grad_pre, axis=0)
    grad_pre_bf = grad_pre.astype(jnp.bfloat16)
    grad_hidden_weight = contract_rows(hidden_two, grad_pre_bf)
    grad_two = lax.psum(contract_cols(grad_pre_bf, hidden_weight), "tensor")
    grad_gain_second = jnp.sum(grad_two * normed_two, axis=0)
    grad_shift_second = jnp.sum(grad_two, axis=0)
    grad_middle = grad_top + norm_backward(grad_two, normed_two, inverse_two, gain_second)
    grad_output_bias = jnp.sum(grad_middle, axis=0)
    grad_middle_bf = grad_middle.astype(jnp.bfloat16)
    grad_attn_output = contract_rows(attended, grad_middle_bf)
    grad_attended = (
        contract_cols(grad_middle_bf, attn_output).astype(jnp.bfloat16).reshape(row_count, -1, HD)
    )
    grad_queries, grad_keys, grad_values = attend_back(
        queries, keys_bf, values_bf, allowed, log_sum, grad_attended
    )
    grad_queries = grad_queries.reshape(row_count, local_width)
    grad_keys = grad_keys.reshape(row_count, local_width)
    grad_values = grad_values.reshape(row_count, local_width)
    grad_query_bias = jnp.sum(grad_queries, axis=0)
    grad_value_bias = jnp.sum(grad_values, axis=0)
    grad_stack = jnp.stack([grad_queries, grad_keys, grad_values]).astype(jnp.bfloat16)
    grad_attn_input = jnp.einsum(
        "rd,trc->tdc", hidden_one, grad_stack, preferred_element_type=jnp.float32
    )
    one_part = jnp.einsum("trc,tdc->rd", grad_stack, attn_input, preferred_element_type=jnp.float32)
    grad_one = lax.psum(one_part, "tensor")
    grad_gain_first = jnp.sum(grad_one * normed_one, axis=0)
    grad_shift_first = jnp.sum(grad_one, axis=0)
    input_grad = (
        grad_middle + norm_backward(grad_one, normed_one, inverse_one, gain_first)
    ).astype(jnp.bfloat16)
    (
        grad_attn_input,
        grad_query_bias,
        grad_value_bias,
        grad_attn_output,
        grad_output_bias,
        grad_gain_first,
        grad_shift_first,
        grad_hidden_weight,
        grad_hidden_bias,
        grad_down_weight,
        grad_down_bias,
        grad_gain_second,
        grad_shift_second,
    ) = lax.psum(
        (
            grad_attn_input,
            grad_query_bias,
            grad_value_bias,
            grad_attn_output,
            grad_output_bias,
            grad_gain_first,
            grad_shift_first,
            grad_hidden_weight,
            grad_hidden_bias,
            grad_down_weight,
            grad_down_bias,
            grad_gain_second,
            grad_shift_second,
        ),
        "dp",
    )
    return (
        block_out,
        input_grad,
        grad_attn_input,
        grad_query_bias,
        grad_value_bias,
        grad_attn_output,
        grad_output_bias,
        grad_gain_first,
        grad_shift_first,
        grad_hidden_weight,
        grad_hidden_bias,
        grad_down_weight,
        grad_down_bias,
        grad_gain_second,
        grad_shift_second,
    )


def shards(
    tokens,
    segment_ids,
    cotangent,
    attn_input,
    query_bias,
    value_bias,
    attn_output,
    output_bias,
    gain_first,
    shift_first,
    hidden_weight,
    hidden_bias,
    down_weight,
    down_bias,
    gain_second,
    shift_second,
):
    if lax.axis_size("tensor") != 4 or lax.axis_size("dp") != 8:
        return plain_shards(
            tokens,
            segment_ids,
            cotangent,
            attn_input,
            query_bias,
            value_bias,
            attn_output,
            output_bias,
            gain_first,
            shift_first,
            hidden_weight,
            hidden_bias,
            down_weight,
            down_bias,
            gain_second,
            shift_second,
        )
    row_count = tokens.shape[0]
    local_width = attn_input.shape[2]
    valid = (segment_ids >= 0)[:, None]
    cot_masked = jnp.where(valid, cotangent, jnp.zeros_like(cotangent))
    allowed = allowed_mask(segment_ids)
    resid_in = tokens.astype(jnp.float32)
    normed_one, inverse_one, pre_one = norm_forward(resid_in, gain_first, shift_first)
    hidden_one = pre_one.astype(jnp.bfloat16)
    projected = jnp.einsum(
        "rd,tdc->trc", hidden_one, attn_input, preferred_element_type=jnp.float32
    )
    queries = (projected[0] + query_bias).astype(jnp.bfloat16).reshape(row_count, -1, HD)
    keys_bf = projected[1].astype(jnp.bfloat16).reshape(row_count, -1, HD)
    values_bf = (projected[2] + value_bias).astype(jnp.bfloat16).reshape(row_count, -1, HD)
    mixed, log_sum = attend(queries, keys_bf, values_bf, allowed)
    attended = mixed.reshape(row_count, local_width).astype(jnp.bfloat16)
    attn_part = jnp.dot(attended, attn_output, preferred_element_type=jnp.float32)
    middle = resid_in + tensor_sum([attn_part], 0)[0] + output_bias
    normed_two, inverse_two, pre_two = norm_forward(middle, gain_second, shift_second)
    hidden_two = pre_two.astype(jnp.bfloat16)
    pre_act = jnp.dot(hidden_two, hidden_weight, preferred_element_type=jnp.float32) + hidden_bias
    gelu_value, gelu_slope = gelu_pair(pre_act)
    activation = gelu_value.astype(jnp.bfloat16)
    mlp_part = jnp.dot(activation, down_weight, preferred_element_type=jnp.float32)
    grad_top = cot_masked.astype(jnp.float32)
    grad_down_bias = jnp.sum(grad_top, axis=0)
    grad_down_weight = contract_rows(activation, cot_masked)
    grad_pre = contract_cols(cot_masked, down_weight) * gelu_slope
    grad_hidden_bias = jnp.sum(grad_pre, axis=0)
    grad_pre_bf = grad_pre.astype(jnp.bfloat16)
    grad_hidden_weight = contract_rows(hidden_two, grad_pre_bf)
    two_part = contract_cols(grad_pre_bf, hidden_weight)
    width = tokens.shape[1]
    heads = local_width // HD
    vectors = jnp.concatenate(
        [gain_first, gain_second, down_bias, grad_hidden_bias, grad_down_bias]
    ).reshape(5, width)
    operands = (
        two_part,
        mlp_part,
        grad_down_weight,
        grad_hidden_weight,
        middle,
        tokens,
        cot_masked,
        hidden_one,
        queries.transpose(1, 0, 2),
        keys_bf.transpose(1, 0, 2),
        values_bf.transpose(1, 0, 2),
        attended,
        attn_output,
        attn_input.transpose(0, 2, 1).reshape(3 * local_width, width),
        segment_ids[:, None],
        segment_ids[None, :],
        jnp.pad(vectors, ((0, 3), (0, 0))),
    )
    block_out, input_grad, grad_down_weight, grad_hidden_weight, attn_mat, small = backward_pass(
        operands, heads, 2
    )
    grad_attn_input = attn_mat[: 3 * local_width].reshape(3, local_width, width).transpose(0, 2, 1)
    grad_attn_output = attn_mat[3 * local_width :]
    (
        grad_hidden_bias,
        grad_down_bias,
        grad_gain_second,
        grad_shift_second,
        grad_output_bias,
        grad_gain_first,
        grad_shift_first,
    ) = (small[r] for r in range(7))
    grad_query_bias = small[8 : 8 + heads, :HD].reshape(local_width)
    grad_value_bias = small[8 + heads : 8 + 2 * heads, :HD].reshape(local_width)
    return (
        block_out,
        input_grad,
        grad_attn_input,
        grad_query_bias,
        grad_value_bias,
        grad_attn_output,
        grad_output_bias,
        grad_gain_first,
        grad_shift_first,
        grad_hidden_weight,
        grad_hidden_bias,
        grad_down_weight,
        grad_down_bias,
        grad_gain_second,
        grad_shift_second,
    )


def solution(mesh):
    return jax.shard_map(
        shards,
        mesh=mesh,
        in_specs=(
            P("dp", None),
            P("dp"),
            P("dp", None),
            P(None, None, "tensor"),
            P("tensor"),
            P("tensor"),
            P("tensor", None),
            P(),
            P(),
            P(),
            P(None, "tensor"),
            P("tensor"),
            P("tensor", None),
            P(),
            P(),
            P(),
        ),
        out_specs=(
            P("dp", None),
            P("dp", None),
            P(None, None, "tensor"),
            P("tensor"),
            P("tensor"),
            P("tensor", None),
            P(),
            P(),
            P(),
            P(None, "tensor"),
            P("tensor"),
            P("tensor", None),
            P(),
            P(),
            P(),
        ),
        check_vma=False,
    )
```

```python
import jax
import jax.numpy as jnp
from jax import lax
from jax.experimental import pallas as pl
from jax.experimental.pallas import tpu as pltpu
from jax.sharding import PartitionSpec as P

HD = 64
MESH = pl.DeviceIdType.MESH
VM = pl.BlockSpec(memory_space=pltpu.VMEM)
LIMIT = 60 * 1024 * 1024
TPIECES = 4
DPIECES = 4


EPSILON = 1e-05
TANH_SCALE = 0.7978845608028654
CUBIC = 0.044715


def norm_forward(values_in, norm_gain, norm_shift):
    row_mean = jnp.mean(values_in, axis=-1, keepdims=True)
    centered = values_in - row_mean
    inverse = lax.rsqrt(jnp.mean(centered * centered, axis=-1, keepdims=True) + EPSILON)
    normed = centered * inverse
    return (normed, inverse, normed * norm_gain + norm_shift)


def norm_backward(grad_out, normed, inverse, norm_gain):
    scaled = grad_out * norm_gain
    return inverse * (
        scaled
        - jnp.mean(scaled, axis=-1, keepdims=True)
        - normed * jnp.mean(scaled * normed, axis=-1, keepdims=True)
    )


def gelu_pair(pre_act):
    tangent = jnp.tanh(TANH_SCALE * (pre_act + CUBIC * pre_act * pre_act * pre_act))
    gelu_value = 0.5 * pre_act * (1.0 + tangent)
    gelu_slope = 0.5 * (1.0 + tangent) + 0.5 * pre_act * (1.0 - tangent * tangent) * TANH_SCALE * (
        1.0 + 3.0 * CUBIC * pre_act * pre_act
    )
    return (gelu_value, gelu_slope)


def contract_rows(left_mat, right_mat):
    return lax.dot_general(
        left_mat, right_mat, (((0,), (0,)), ((), ())), preferred_element_type=jnp.float32
    )


def contract_cols(left_mat, right_mat):
    return lax.dot_general(
        left_mat, right_mat, (((1,), (1,)), ((), ())), preferred_element_type=jnp.float32
    )


def allowed_mask(segments):
    position = jnp.arange(segments.shape[0])
    return (segments[:, None] == segments[None, :]) & (position[None, :] <= position[:, None])


def head_scores(queries, keys_bf, allowed):
    scaling = queries.shape[-1] ** (-0.5)
    scores = (
        jnp.einsum("qhd,khd->hqk", queries, keys_bf, preferred_element_type=jnp.float32) * scaling
    )
    return jnp.where(allowed[None], scores, -jnp.inf)


def attend(queries, keys_bf, values_bf, allowed):
    scores = head_scores(queries, keys_bf, allowed)
    top_score = jnp.max(scores, axis=-1, keepdims=True)
    log_sum = top_score + jnp.log(jnp.sum(jnp.exp(scores - top_score), axis=-1, keepdims=True))
    probs = jnp.exp(scores - log_sum).astype(jnp.bfloat16)
    mixed = jnp.einsum("hqk,khd->qhd", probs, values_bf, preferred_element_type=jnp.float32)
    return (mixed, log_sum)


def attend_back(queries, keys_bf, values_bf, allowed, log_sum, grad_mixed):
    probs_full = jnp.exp(head_scores(queries, keys_bf, allowed) - log_sum)
    probs_bf = probs_full.astype(jnp.bfloat16)
    grad_values = jnp.einsum(
        "hqk,qhd->khd", probs_bf, grad_mixed, preferred_element_type=jnp.float32
    )
    grad_probs = jnp.einsum(
        "qhd,khd->hqk", grad_mixed, values_bf, preferred_element_type=jnp.float32
    )
    scaling = queries.shape[-1] ** (-0.5)
    grad_scores = (
        probs_full
        * (grad_probs - jnp.sum(probs_full * grad_probs, axis=-1, keepdims=True))
        * scaling
    ).astype(jnp.bfloat16)
    grad_queries = jnp.einsum(
        "hqk,khd->qhd", grad_scores, keys_bf, preferred_element_type=jnp.float32
    )
    grad_keys = jnp.einsum("hqk,qhd->khd", grad_scores, queries, preferred_element_type=jnp.float32)
    return (grad_queries, grad_keys, grad_values)


def push(src, dst, send_sem, recv_sem, device):
    copy = pltpu.make_async_remote_copy(
        src_ref=src,
        dst_ref=dst,
        send_sem=send_sem,
        recv_sem=recv_sem,
        device_id=device,
        device_id_type=MESH,
    )
    copy.start()
    return copy


def tensor_scratch(count, rows, width):
    piece = rows // 2 // TPIECES
    buf = pltpu.VMEM((count * TPIECES, piece, width), jnp.float32)
    sem = pltpu.SemaphoreType.DMA((count * TPIECES,))
    return [buf] * 5 + [sem] * 6


class TensorSum:
    def __init__(self, parts, outs, scratch):
        self.parts, self.outs = parts, outs
        self.rx, self.mid, self.ry, self.fin, self.rb = scratch[:5]
        self.sems = scratch[5:11]
        dp = lax.axis_index("dp")
        me = lax.axis_index("tensor")
        low = me % 2
        self.near = (dp, me + 1 - 2 * low)
        self.far = (dp, me + 2 - 4 * (me // 2))
        half = parts[0].shape[0] // 2
        self.piece = half // TPIECES
        self.mine, self.other = low * half, (1 - low) * half
        self.units = [(a, k) for a in range(len(parts)) for k in range(TPIECES)]
        self.copies = [[], [], []]

    def peers(self):
        return [self.near, self.far]

    def window(self, base, k):
        return pl.ds(pl.multiple_of(base + k * self.piece, 8), self.piece)

    def send_halves(self):
        for u, (a, k) in enumerate(self.units):
            src = self.parts[a].at[self.window(self.other, k)]
            self.copies[0].append(
                push(src, self.rx.at[u], self.sems[0].at[u], self.sems[1].at[u], self.near)
            )

    def cross(self, u):
        a, k = self.units[u]
        self.copies[0][u].wait_recv()
        self.mid[u] = self.parts[a][self.window(self.mine, k)] + self.rx[u]
        self.copies[1].append(
            push(self.mid.at[u], self.ry.at[u], self.sems[2].at[u], self.sems[3].at[u], self.far)
        )

    def finish(self, u):
        a, k = self.units[u]
        self.copies[1][u].wait_recv()
        total = self.mid[u] + self.ry[u]
        self.fin[u] = total
        self.outs[a][self.window(self.mine, k)] = total
        self.copies[2].append(
            push(self.fin.at[u], self.rb.at[u], self.sems[4].at[u], self.sems[5].at[u], self.near)
        )

    def collect(self, u):
        a, k = self.units[u]
        self.copies[2][u].wait_recv()
        self.outs[a][self.window(self.other, k)] = self.rb[u]

    def drain(self):
        for group in self.copies:
            for copy in group:
                copy.wait_send()


def greet(peers):
    barrier = pltpu.get_barrier_semaphore()
    for peer in peers:
        pl.semaphore_signal(barrier, inc=1, device_id=peer, device_id_type=MESH)
    pl.semaphore_wait(barrier, len(peers))


def tensor_kernel(count, *refs):
    parts, outs, scratch = refs[:count], refs[count : 2 * count], refs[2 * count :]
    job = TensorSum(parts, outs, scratch)
    greet(job.peers())
    job.send_halves()
    for u in range(len(job.units)):
        job.cross(u)
    for u in range(len(job.units)):
        job.finish(u)
    for u in range(len(job.units)):
        job.collect(u)
    job.drain()


def tensor_sum(parts, number):
    rows, width = parts[0].shape
    if lax.axis_size("tensor") != 4:
        return lax.psum(parts, "tensor")
    return pl.pallas_call(
        lambda *refs: tensor_kernel(len(parts), *refs),
        out_shape=[jax.ShapeDtypeStruct((rows, width), jnp.float32)] * len(parts),
        in_specs=[VM] * len(parts),
        out_specs=[VM] * len(parts),
        scratch_shapes=tensor_scratch(len(parts), rows, width),
        compiler_params=pltpu.CompilerParams(
            collective_id=number, has_side_effects=True, vmem_limit_bytes=LIMIT
        ),
        name="tensor_sum",
    )(*parts)


def dot(left, right, left_dim, right_dim):
    return lax.dot_general(
        left, right, (((left_dim,), (right_dim,)), ((), ())), preferred_element_type=jnp.float32
    )


def backward_kernel(heads, *refs):
    (two_part, mlp_part, down_mat, hidden_mat, middle, tokens, cot, hidden_one, queries, keys, values) = refs[:11]
    (attended, attn_output, attn_rows, seg_col, seg_row, vectors) = refs[11:17]
    block_out, input_grad, down_out, hidden_out, attn_out, small_out = refs[17:23]
    two_sum, mlp_sum, one_part, one_sum, attn_mat, grad_middle = refs[23:29]
    job_two = TensorSum([two_part], [two_sum], refs[29:40])
    job_mlp = TensorSum([mlp_part], [mlp_sum], refs[40:51])
    job_one = TensorSum([one_part], [one_sum], refs[51:62])
    rx, own, rz, ry, rg = refs[62:67]
    sx, qx, sz, qz, sy, qy, sg, qg = refs[67:75]
    slots, mine_small, ss, qs = refs[75:79]
    edge_in, sums, mid_in, side_in, mid_back = refs[79:84]
    s_in, q_in, s_mid, q_mid, s_side, q_side, s_back, q_back, s_near, q_near, s_rest, q_rest = refs[84:96]
    mats, outs = [down_mat, hidden_mat, attn_mat], [down_out, hidden_out, attn_out]

    dp = lax.axis_index("dp")
    me = lax.axis_index("tensor")
    column, line = dp % 2, dp // 2
    inner = (line == 1) | (line == 2)
    edge = (line == 0) | (line == 3)
    across = (dp + 1 - 2 * column, me)
    odd = line % 2
    beside = ((line + 1 - 2 * odd) * 2 + column, me)
    middle_peer = ((2 - line // 2) * 2 + column, me)
    peers = [((dp + j) % 8, me) for j in range(1, 8)]
    full = down_mat.shape[0] // DPIECES
    piece = full // 2
    upper = line // 2
    halves = DPIECES // 2
    units = [(1, k) for k in range(DPIECES)] + [(2, k) for k in range(halves)]
    line_units = [(0, k) for k in range(DPIECES)] + [(2, k) for k in range(halves, DPIECES)]
    count = len(units)

    def window(index, k):
        return pl.ds(pl.multiple_of(k * full + index * piece, 8), piece)

    def part(index):
        return pl.ds(pl.multiple_of(index * piece, 8), piece)

    def remote(src, dst, send, recv, device):
        return pltpu.make_async_remote_copy(
            src_ref=src,
            dst_ref=dst,
            send_sem=send,
            recv_sem=recv,
            device_id=device,
            device_id_type=MESH,
        )

    def to_across(u):
        m, k = units[u]
        src = mats[m].at[window(1 - column, k)]
        return remote(src, rx.at[u], sx.at[u], qx.at[u], across)

    def to_beside(u, src):
        return remote(src, rz.at[u], sz.at[u], qz.at[u], beside)

    def between_middles(u):
        return remote(own.at[u], ry.at[u], sy.at[u], qy.at[u], middle_peer)

    def give_back(u, src):
        return remote(src, rg.at[u], sg.at[u], qg.at[u], across)

    def done(u):
        m, k = units[u]
        return outs[m].at[window(column, k)]

    def stage_a(u):
        m, k = units[u]
        to_across(u).wait_recv()
        own[u] = mats[m][window(column, k)] + rx[u]

        @pl.when(edge)
        def _():
            to_beside(u, own.at[u]).start()

    def stage_b(u):
        @pl.when(inner)
        def _():
            to_beside(u, own.at[u]).wait_recv()
            own[u] = own[u] + rz[u]
            between_middles(u).start()

    def stage_c(u):
        m, k = units[u]

        @pl.when(inner)
        def _():
            between_middles(u).wait_recv()
            outs[m][window(column, k)] = own[u] + ry[u]
            to_beside(u, done(u)).start()
            give_back(u, done(u)).start()

    def stage_d(u):
        m, k = units[u]

        @pl.when(edge)
        def _():
            to_beside(u, own.at[u]).wait_recv()
            give_back(u, rz.at[u]).start()
            outs[m][window(column, k)] = rz[u]

    def stage_e(u):
        m, k = units[u]
        give_back(u, own.at[u]).wait_recv()
        outs[m][window(1 - column, k)] = rg[u]

    def line_in(u):
        m, k = line_units[u]
        src = mats[m].at[k * full : (k + 1) * full]
        return remote(src, edge_in.at[u], s_in.at[u], q_in.at[u], beside)

    def line_mid(u):
        src = sums.at[u, part(1 - upper)]
        return remote(src, mid_in.at[u], s_mid.at[u], q_mid.at[u], middle_peer)

    def line_side(u):
        src = sums.at[u, part(upper)]
        return remote(src, side_in.at[u], s_side.at[u], q_side.at[u], across)

    def line_done(u):
        m, k = line_units[u]
        return outs[m].at[window(upper, k)]

    def line_back(u):
        return remote(line_done(u), mid_back.at[u], s_back.at[u], q_back.at[u], middle_peer)

    def line_near(u):
        dst = edge_in.at[u, part(upper)]
        return remote(line_done(u), dst, s_near.at[u], q_near.at[u], beside)

    def line_rest(u):
        dst = edge_in.at[u, part(1 - upper)]
        return remote(mid_back.at[u], dst, s_rest.at[u], q_rest.at[u], beside)

    def line_b(u):
        m, k = line_units[u]

        @pl.when(inner)
        def _():
            line_in(u).wait_recv()
            sums[u] = mats[m][k * full : (k + 1) * full] + edge_in[u]
            line_mid(u).start()

    def line_c(u):
        @pl.when(inner)
        def _():
            line_mid(u).wait_recv()
            sums[u, part(upper)] = sums[u, part(upper)] + mid_in[u]
            line_side(u).start()

    def line_d(u):
        m, k = line_units[u]

        @pl.when(inner)
        def _():
            line_side(u).wait_recv()
            outs[m][window(upper, k)] = sums[u, part(upper)] + side_in[u]
            line_back(u).start()
            line_near(u).start()

    def line_e(u):
        m, k = line_units[u]

        @pl.when(inner)
        def _():
            line_back(u).wait_recv()
            line_rest(u).start()
            outs[m][window(1 - upper, k)] = mid_back[u]

    def line_f(u):
        m, k = line_units[u]

        @pl.when(edge)
        def _():
            line_near(u).wait_recv()
            line_rest(u).wait_recv()
            outs[m][k * full : (k + 1) * full] = edge_in[u]

    stages = [stage_a, stage_b, stage_c, stage_d, None]
    line_stages = [line_b, line_c, line_d, line_e, line_f]

    def step(at):
        for lag in range(len(stages)):
            if 0 <= at - lag < count:
                line_stages[lag](at - lag)
                if stages[lag] is not None:
                    stages[lag](at - lag)

    def line_starts(first, last):
        @pl.when(edge)
        def _():
            for u in range(first, last):
                line_in(u).start()

    def each(call, job):
        for u in range(len(job.units)):
            call(u)

    greet(peers + job_two.peers())
    job_two.send_halves()
    job_mlp.send_halves()
    for u in range(DPIECES):
        to_across(u).start()
    line_starts(0, DPIECES)
    each(job_two.cross, job_two)
    each(job_mlp.cross, job_mlp)
    each(job_two.finish, job_two)
    each(job_two.collect, job_two)

    gain_first, gain_second, down_bias = vectors[0:1, :], vectors[1:2, :], vectors[2:3, :]
    normed_two, inverse_two, _ = norm_forward(middle[...], gain_second, 0.0)
    grad_two = two_sum[...]
    mine_small[...] = jnp.zeros_like(mine_small)
    mine_small[0:2, :] = vectors[3:5, :]
    mine_small[2:3, :] = jnp.sum(grad_two * normed_two, axis=0, keepdims=True)
    mine_small[3:4, :] = jnp.sum(grad_two, axis=0, keepdims=True)
    grad_mid = cot[...].astype(jnp.float32) + norm_backward(
        grad_two, normed_two, inverse_two, gain_second
    )
    grad_middle[...] = grad_mid
    mine_small[4:5, :] = jnp.sum(grad_mid, axis=0, keepdims=True)
    mid_bf = grad_mid.astype(jnp.bfloat16)
    row_count, local_width = attended.shape
    attn_mat[3 * local_width :, :] = dot(attended[...], mid_bf, 0, 0)
    step(0)

    row_at = lax.broadcasted_iota(jnp.int32, (row_count, row_count), 0)
    col_at = lax.broadcasted_iota(jnp.int32, (row_count, row_count), 1)
    allowed = (seg_col[...] == seg_row[...]) & (col_at <= row_at)
    scaling = HD ** (-0.5)
    normal = hidden_one[...]
    for h in range(heads):
        query, key, value = queries[h], keys[h], values[h]
        scores = jnp.where(allowed, dot(query, key, 1, 1) * scaling, -jnp.inf)
        top = jnp.max(scores, axis=-1, keepdims=True)
        log_sum = top + jnp.log(jnp.sum(jnp.exp(scores - top), axis=-1, keepdims=True))
        probs = jnp.exp(scores - log_sum)
        grad_mixed = dot(mid_bf, attn_output[h * HD : (h + 1) * HD, :], 1, 1).astype(jnp.bfloat16)
        grad_value = dot(probs.astype(jnp.bfloat16), grad_mixed, 0, 0)
        grad_probs = dot(grad_mixed, value, 1, 1)
        weighted = jnp.sum(probs * grad_probs, axis=-1, keepdims=True)
        grad_scores = (probs * (grad_probs - weighted) * scaling).astype(jnp.bfloat16)
        grad_query = dot(grad_scores, key, 1, 0)
        grad_key = dot(grad_scores, query, 0, 0)
        mine_small[8 + h : 9 + h, 0:HD] = jnp.sum(grad_query, axis=0, keepdims=True)
        mine_small[8 + heads + h : 9 + heads + h, 0:HD] = jnp.sum(grad_value, axis=0, keepdims=True)
        for m, item in enumerate((grad_query, grad_key, grad_value)):
            item = item.astype(jnp.bfloat16)
            start = m * local_width + h * HD
            attn_mat[start : start + HD, :] = dot(item, normal, 0, 0)
            term = dot(item, attn_rows[start : start + HD, :], 1, 0)
            if h == 0 and m == 0:
                one_part[...] = term
            else:
                one_part[...] += term
    for u in range(DPIECES, count):
        to_across(u).start()
    line_starts(DPIECES, count)
    job_one.send_halves()
    at = 1
    step(at)
    each(job_one.cross, job_one)
    each(job_mlp.finish, job_mlp)
    step(at + 1)
    each(job_one.finish, job_one)
    each(job_mlp.collect, job_mlp)
    valid = seg_col[...] >= 0
    out_full = middle[...] + mlp_sum[...] + down_bias
    block_out[...] = jnp.where(valid, out_full, 0.0).astype(block_out.dtype)
    step(at + 2)
    each(job_one.collect, job_one)
    normed_one, inverse_one, _ = norm_forward(tokens[...].astype(jnp.float32), gain_first, 0.0)
    grad_one = one_sum[...]
    mine_small[5:6, :] = jnp.sum(grad_one * normed_one, axis=0, keepdims=True)
    mine_small[6:7, :] = jnp.sum(grad_one, axis=0, keepdims=True)
    slots[dp] = mine_small[...]
    notes = []
    for j, peer in enumerate(peers):
        notes.append(push(mine_small, slots.at[dp], ss.at[j], qs.at[j], peer))
    step(at + 3)
    back = norm_backward(grad_one, normed_one, inverse_one, gain_first)
    input_grad[...] = (grad_middle[...] + back).astype(input_grad.dtype)
    for i in range(at + 4, count + len(stages) - 1):
        step(i)
    for note in notes:
        note.wait_recv()
    total = slots[0]
    for j in range(1, 8):
        total = total + slots[j]
    small_out[...] = total
    for u in range(count):
        stage_e(u)

    for job in (job_two, job_mlp, job_one):
        job.drain()
    for note in notes:
        note.wait_send()
    for u in range(count):
        to_across(u).wait_send()
        to_beside(u, own.at[u]).wait_send()
        give_back(u, own.at[u]).wait_send()

    @pl.when(edge)
    def _():
        for u in range(count):
            line_in(u).wait_send()

    @pl.when(inner)
    def _():
        for u in range(count):
            between_middles(u).wait_send()
            line_mid(u).wait_send()
            line_side(u).wait_send()
            line_back(u).wait_send()
            line_near(u).wait_send()
            line_rest(u).wait_send()


def backward_pass(operands, heads, number):
    rows, width = operands[0].shape
    square = jax.ShapeDtypeStruct((width, width), jnp.float32)
    small = (16, width)
    whole = pltpu.VMEM((rows, width), jnp.float32)
    count = 3 * DPIECES // 2
    buf = pltpu.VMEM((count, width // 2 // DPIECES, width), jnp.float32)
    wide = pltpu.VMEM((count, width // DPIECES, width), jnp.float32)
    sem = pltpu.SemaphoreType.DMA((count,))
    tile = jax.ShapeDtypeStruct((rows, width), jnp.bfloat16)
    return pl.pallas_call(
        lambda *refs: backward_kernel(heads, *refs),
        out_shape=[tile, tile, square, square, square, jax.ShapeDtypeStruct(small, jnp.float32)],
        in_specs=[VM] * len(operands),
        out_specs=[VM] * 6,
        scratch_shapes=[whole] * 4
        + [pltpu.VMEM((width, width), jnp.float32), whole]
        + tensor_scratch(1, rows, width) * 3
        + [buf] * 5
        + [sem] * 8
        + [
            pltpu.VMEM((8, *small), jnp.float32),
            pltpu.VMEM(small, jnp.float32),
            pltpu.SemaphoreType.DMA((7,)),
            pltpu.SemaphoreType.DMA((7,)),
        ]
        + [wide, wide, buf, buf, buf]
        + [sem] * 12,
        compiler_params=pltpu.CompilerParams(
            collective_id=number, has_side_effects=True, vmem_limit_bytes=67043328
        ),
        name="backward_pass",
    )(*operands)


def plain_shards(
    tokens,
    segment_ids,
    cotangent,
    attn_input,
    query_bias,
    value_bias,
    attn_output,
    output_bias,
    gain_first,
    shift_first,
    hidden_weight,
    hidden_bias,
    down_weight,
    down_bias,
    gain_second,
    shift_second,
):
    row_count = tokens.shape[0]
    local_width = attn_input.shape[2]
    valid = (segment_ids >= 0)[:, None]
    cot_masked = jnp.where(valid, cotangent, jnp.zeros_like(cotangent))
    allowed = allowed_mask(segment_ids)
    resid_in = tokens.astype(jnp.float32)
    normed_one, inverse_one, pre_one = norm_forward(resid_in, gain_first, shift_first)
    hidden_one = pre_one.astype(jnp.bfloat16)
    projected = jnp.einsum(
        "rd,tdc->trc", hidden_one, attn_input, preferred_element_type=jnp.float32
    )
    queries = (projected[0] + query_bias).astype(jnp.bfloat16).reshape(row_count, -1, HD)
    keys_bf = projected[1].astype(jnp.bfloat16).reshape(row_count, -1, HD)
    values_bf = (projected[2] + value_bias).astype(jnp.bfloat16).reshape(row_count, -1, HD)
    mixed, log_sum = attend(queries, keys_bf, values_bf, allowed)
    attended = mixed.reshape(row_count, local_width).astype(jnp.bfloat16)
    attn_part = jnp.dot(attended, attn_output, preferred_element_type=jnp.float32)
    middle = resid_in + lax.psum(attn_part, "tensor") + output_bias
    normed_two, inverse_two, pre_two = norm_forward(middle, gain_second, shift_second)
    hidden_two = pre_two.astype(jnp.bfloat16)
    pre_act = jnp.dot(hidden_two, hidden_weight, preferred_element_type=jnp.float32) + hidden_bias
    gelu_value, gelu_slope = gelu_pair(pre_act)
    activation = gelu_value.astype(jnp.bfloat16)
    mlp_part = jnp.dot(activation, down_weight, preferred_element_type=jnp.float32)
    out_full = middle + lax.psum(mlp_part, "tensor") + down_bias
    block_out = jnp.where(valid, out_full, jnp.zeros_like(out_full)).astype(jnp.bfloat16)
    grad_top = cot_masked.astype(jnp.float32)
    grad_down_bias = jnp.sum(grad_top, axis=0)
    grad_down_weight = contract_rows(activation, cot_masked)
    grad_pre = contract_cols(cot_masked, down_weight) * gelu_slope
    grad_hidden_bias = jnp.sum(grad_pre, axis=0)
    grad_pre_bf = grad_pre.astype(jnp.bfloat16)
    grad_hidden_weight = contract_rows(hidden_two, grad_pre_bf)
    grad_two = lax.psum(contract_cols(grad_pre_bf, hidden_weight), "tensor")
    grad_gain_second = jnp.sum(grad_two * normed_two, axis=0)
    grad_shift_second = jnp.sum(grad_two, axis=0)
    grad_middle = grad_top + norm_backward(grad_two, normed_two, inverse_two, gain_second)
    grad_output_bias = jnp.sum(grad_middle, axis=0)
    grad_middle_bf = grad_middle.astype(jnp.bfloat16)
    grad_attn_output = contract_rows(attended, grad_middle_bf)
    grad_attended = (
        contract_cols(grad_middle_bf, attn_output).astype(jnp.bfloat16).reshape(row_count, -1, HD)
    )
    grad_queries, grad_keys, grad_values = attend_back(
        queries, keys_bf, values_bf, allowed, log_sum, grad_attended
    )
    grad_queries = grad_queries.reshape(row_count, local_width)
    grad_keys = grad_keys.reshape(row_count, local_width)
    grad_values = grad_values.reshape(row_count, local_width)
    grad_query_bias = jnp.sum(grad_queries, axis=0)
    grad_value_bias = jnp.sum(grad_values, axis=0)
    grad_stack = jnp.stack([grad_queries, grad_keys, grad_values]).astype(jnp.bfloat16)
    grad_attn_input = jnp.einsum(
        "rd,trc->tdc", hidden_one, grad_stack, preferred_element_type=jnp.float32
    )
    one_part = jnp.einsum("trc,tdc->rd", grad_stack, attn_input, preferred_element_type=jnp.float32)
    grad_one = lax.psum(one_part, "tensor")
    grad_gain_first = jnp.sum(grad_one * normed_one, axis=0)
    grad_shift_first = jnp.sum(grad_one, axis=0)
    input_grad = (
        grad_middle + norm_backward(grad_one, normed_one, inverse_one, gain_first)
    ).astype(jnp.bfloat16)
    (
        grad_attn_input,
        grad_query_bias,
        grad_value_bias,
        grad_attn_output,
        grad_output_bias,
        grad_gain_first,
        grad_shift_first,
        grad_hidden_weight,
        grad_hidden_bias,
        grad_down_weight,
        grad_down_bias,
        grad_gain_second,
        grad_shift_second,
    ) = lax.psum(
        (
            grad_attn_input,
            grad_query_bias,
            grad_value_bias,
            grad_attn_output,
            grad_output_bias,
            grad_gain_first,
            grad_shift_first,
            grad_hidden_weight,
            grad_hidden_bias,
            grad_down_weight,
            grad_down_bias,
            grad_gain_second,
            grad_shift_second,
        ),
        "dp",
    )
    return (
        block_out,
        input_grad,
        grad_attn_input,
        grad_query_bias,
        grad_value_bias,
        grad_attn_output,
        grad_output_bias,
        grad_gain_first,
        grad_shift_first,
        grad_hidden_weight,
        grad_hidden_bias,
        grad_down_weight,
        grad_down_bias,
        grad_gain_second,
        grad_shift_second,
    )


def shards(
    tokens,
    segment_ids,
    cotangent,
    attn_input,
    query_bias,
    value_bias,
    attn_output,
    output_bias,
    gain_first,
    shift_first,
    hidden_weight,
    hidden_bias,
    down_weight,
    down_bias,
    gain_second,
    shift_second,
):
    if lax.axis_size("tensor") != 4 or lax.axis_size("dp") != 8:
        return plain_shards(
            tokens,
            segment_ids,
            cotangent,
            attn_input,
            query_bias,
            value_bias,
            attn_output,
            output_bias,
            gain_first,
            shift_first,
            hidden_weight,
            hidden_bias,
            down_weight,
            down_bias,
            gain_second,
            shift_second,
        )
    row_count = tokens.shape[0]
    local_width = attn_input.shape[2]
    valid = (segment_ids >= 0)[:, None]
    cot_masked = jnp.where(valid, cotangent, jnp.zeros_like(cotangent))
    allowed = allowed_mask(segment_ids)
    resid_in = tokens.astype(jnp.float32)
    normed_one, inverse_one, pre_one = norm_forward(resid_in, gain_first, shift_first)
    hidden_one = pre_one.astype(jnp.bfloat16)
    projected = jnp.einsum(
        "rd,tdc->trc", hidden_one, attn_input, preferred_element_type=jnp.float32
    )
    queries = (projected[0] + query_bias).astype(jnp.bfloat16).reshape(row_count, -1, HD)
    keys_bf = projected[1].astype(jnp.bfloat16).reshape(row_count, -1, HD)
    values_bf = (projected[2] + value_bias).astype(jnp.bfloat16).reshape(row_count, -1, HD)
    mixed, log_sum = attend(queries, keys_bf, values_bf, allowed)
    attended = mixed.reshape(row_count, local_width).astype(jnp.bfloat16)
    attn_part = jnp.dot(attended, attn_output, preferred_element_type=jnp.float32)
    middle = resid_in + tensor_sum([attn_part], 0)[0] + output_bias
    normed_two, inverse_two, pre_two = norm_forward(middle, gain_second, shift_second)
    hidden_two = pre_two.astype(jnp.bfloat16)
    pre_act = jnp.dot(hidden_two, hidden_weight, preferred_element_type=jnp.float32) + hidden_bias
    gelu_value, gelu_slope = gelu_pair(pre_act)
    activation = gelu_value.astype(jnp.bfloat16)
    mlp_part = jnp.dot(activation, down_weight, preferred_element_type=jnp.float32)
    grad_top = cot_masked.astype(jnp.float32)
    grad_down_bias = jnp.sum(grad_top, axis=0)
    grad_down_weight = contract_rows(activation, cot_masked)
    grad_pre = contract_cols(cot_masked, down_weight) * gelu_slope
    grad_hidden_bias = jnp.sum(grad_pre, axis=0)
    grad_pre_bf = grad_pre.astype(jnp.bfloat16)
    grad_hidden_weight = contract_rows(hidden_two, grad_pre_bf)
    two_part = contract_cols(grad_pre_bf, hidden_weight)
    width = tokens.shape[1]
    heads = local_width // HD
    vectors = jnp.concatenate(
        [gain_first, gain_second, down_bias, grad_hidden_bias, grad_down_bias]
    ).reshape(5, width)
    operands = (
        two_part,
        mlp_part,
        grad_down_weight,
        grad_hidden_weight,
        middle,
        tokens,
        cot_masked,
        hidden_one,
        queries.transpose(1, 0, 2),
        keys_bf.transpose(1, 0, 2),
        values_bf.transpose(1, 0, 2),
        attended,
        attn_output,
        attn_input.transpose(0, 2, 1).reshape(3 * local_width, width),
        segment_ids[:, None],
        segment_ids[None, :],
        jnp.pad(vectors, ((0, 3), (0, 0))),
    )
    block_out, input_grad, grad_down_weight, grad_hidden_weight, attn_mat, small = backward_pass(
        operands, heads, 2
    )
    grad_attn_input = attn_mat[: 3 * local_width].reshape(3, local_width, width).transpose(0, 2, 1)
    grad_attn_output = attn_mat[3 * local_width :]
    (
        grad_hidden_bias,
        grad_down_bias,
        grad_gain_second,
        grad_shift_second,
        grad_output_bias,
        grad_gain_first,
        grad_shift_first,
    ) = (small[r] for r in range(7))
    grad_query_bias = small[8 : 8 + heads, :HD].reshape(local_width)
    grad_value_bias = small[8 + heads : 8 + 2 * heads, :HD].reshape(local_width)
    return (
        block_out,
        input_grad,
        grad_attn_input,
        grad_query_bias,
        grad_value_bias,
        grad_attn_output,
        grad_output_bias,
        grad_gain_first,
        grad_shift_first,
        grad_hidden_weight,
        grad_hidden_bias,
        grad_down_weight,
        grad_down_bias,
        grad_gain_second,
        grad_shift_second,
    )


def solution(mesh):
    return jax.shard_map(
        shards,
        mesh=mesh,
        in_specs=(
            P("dp", None),
            P("dp"),
            P("dp", None),
            P(None, None, "tensor"),
            P("tensor"),
            P("tensor"),
            P("tensor", None),
            P(),
            P(),
            P(),
            P(None, "tensor"),
            P("tensor"),
            P("tensor", None),
            P(),
            P(),
            P(),
        ),
        out_specs=(
            P("dp", None),
            P("dp", None),
            P(None, None, "tensor"),
            P("tensor"),
            P("tensor"),
            P("tensor", None),
            P(),
            P(),
            P(),
            P(None, "tensor"),
            P("tensor"),
            P("tensor", None),
            P(),
            P(),
            P(),
        ),
        check_vma=False,
    )
```
